1024 devices in a mesh: grp: 4 (over z_lo), gx: 16 (over z_hi, y), gy: 16 (over x, core).
Axes of the slice: x: 8, y: 8, z: 8 (z_hi: 2, z_lo: 4; z = z_hi * 4 + z_lo), core: 2. Of those that a mesh axis runs over, the one named last changes fastest.
Arguments:
- tracers: float32 [19, 32, 32, 8192], P(None, None, 'gy', ('grp', 'gx')), may hold values from 0.1 to 2
- flow: float32 [3, 32, 32, 8192], P(None, None, 'gy', ('grp', 'gx')), may hold values from -0.3 to 0.3
- temp_salt: float32 [2, 32, 32, 8192], P(None, None, 'gy', ('grp', 'gx')), may hold values from -4 to 4
- wet: int32 [32, 32, 8192], P(None, 'gy', ('grp', 'gx')), may hold values from 0 to 1, as said below
Outputs:
- tracers_next: float32 [19, 32, 32, 8192], P(None, None, 'gy', ('grp', 'gx'))
- temp_salt_next: float32 [2, 32, 32, 8192], P(None, None, 'gy', ('grp', 'gx'))
- flow_next: float32 [2, 32, 32, 8192], P(None, None, 'gy', ('grp', 'gx'))
The draws below stay inside these ranges and needn't reach their ends.
Inputs may be any that keep to these rules, and one draw needn't show every extreme that they name: Each water column is wet from the surface down to its own bottom: a cell is 1 only if the cell above it is 1.
All inputs are finite; a program needn't handle non-finite values.
Results may differ from the reference program's by a relative error of at most 0.00002.
Values sent between devices are 32-bit elements; how exact they have to be, the bound alone decides.
A program may use at most 32 MiB of HBM per device.

```python
import math
import jax
import jax.numpy as jnp
from jax import lax

NZ = 32
NTR = 19
SUBSTEPS = 4
NX = 8192
NY = 32


def draw_wet(key, part):
    bottom = jax.random.randint(key, (NY, NX), 0, NZ + 1)
    levels = lax.broadcasted_iota(jnp.int32, (NZ, NY, NX), 0)
    return (levels < bottom[None]).astype(jnp.int32)


def block_scale(stream_key, shape, split, least, high):
    factor_of, own = 1.0, jax.random.fold_in(stream_key, 6)
    for dim, shards_of in split:
        heights = jnp.exp(jax.random.uniform(jax.random.fold_in(own, dim), (shards_of,), jnp.float32, least / len(split), high / len(split)))
        factor_of = factor_of * jnp.repeat(heights, shape[dim] // shards_of).reshape([-1 if axis == dim else 1 for axis in range(len(shape))])
    return factor_of


def bell_draw(key, extent, width, most, shards=(), kind=jnp.bfloat16):
    level = block_scale(key, extent, shards, -0.22, 0.18) if shards else 1.0
    entries = jax.random.normal(key, extent, jnp.float32) * width * level
    return jnp.minimum(jnp.maximum(entries, -most), most).astype(kind)


def setup_inputs(seed: int = 0) -> dict:
    arg_keys = jax.random.split(jax.random.key(seed), 5)
    tracers = jnp.clip(jnp.exp(math.log(2.0) - 2.9957323 * jax.random.uniform(arg_keys[0], (NTR, NZ, NY, NX), jnp.float32) ** block_scale(arg_keys[0], (NTR, NZ, NY, NX), ((2, 16), (3, 64)), -0.2, 0.2)), 0.1, 2.0)
    flow = jnp.clip(jax.random.uniform(arg_keys[1], (3, NZ, NY, NX), jnp.float32, -0.3, 0.3) * block_scale(arg_keys[1], (3, NZ, NY, NX), ((2, 16), (3, 64)), -0.4, 0.0), -0.3, 0.3)
    temp_salt = bell_draw(arg_keys[2], (2, NZ, NY, NX), 1.0, 4.0, ((2, 16), (3, 64)), jnp.float32)
    wet = draw_wet(jax.random.fold_in(arg_keys[4], 71), 0)
    return dict(tracers=tracers, flow=flow, temp_salt=temp_salt, wet=wet)


light_water = 0.04
light_chloro = 0.06
rho_temp = -0.2
rho_salt = 0.8
time_step = 0.02
coriolis = 0.4
viscosity = 0.1
heat_gain = 4.0
photic_halfway_level = 0.2
highest_division_speed = 1.5
half_nutrient = 0.5
half_prey = 0.3
phyto_loss = 0.05
zoo_loss = 0.1
graze_yield = 0.3
remin_rate = 0.15
bio_step = 0.25
thermal_multiplier = 0.063


def minmod(former, latter):
    return jnp.maximum(jnp.minimum(former, latter), 0.0) + jnp.minimum(jnp.maximum(former, latter), 0.0)


def inner_slice(values, direction, lower_end, upper_end):
    dim_count = values.ndim
    selector = []
    for dimension in range(dim_count):
        spatial = dimension - (dim_count - 3)
        if spatial == direction:
            selector.append(slice(lower_end, upper_end))
        elif spatial >= 0:
            selector.append(slice(2, values.shape[dimension] - 2))
        else:
            selector.append(slice(None))
    return values[tuple(selector)]


def advect(scalars, courant, wet_ext):
    change = jnp.zeros_like(inner_slice(scalars, 3, 0, 0))
    for direction in range(3):
        cut_dim = scalars.ndim - 3 + direction
        length = scalars.shape[cut_dim]
        centre = inner_slice(scalars, direction, 1, length - 1)
        forward = inner_slice(scalars, direction, 2, length) - centre
        backward = centre - inner_slice(scalars, direction, 0, length - 2)
        slopes = minmod(forward, backward)
        velocity = courant[direction]
        face_speed = 0.5 * (inner_slice(velocity, direction, 1, length - 2) + inner_slice(velocity, direction, 2, length - 1))
        face_speed = face_speed * inner_slice(wet_ext, direction, 1, length - 2) * inner_slice(wet_ext, direction, 2, length - 1)
        left_value = lax.slice_in_dim(centre, 0, length - 3, axis=cut_dim)
        right_value = lax.slice_in_dim(centre, 1, length - 2, axis=cut_dim)
        left_slope = lax.slice_in_dim(slopes, 0, length - 3, axis=cut_dim)
        right_slope = lax.slice_in_dim(slopes, 1, length - 2, axis=cut_dim)
        flux = jnp.maximum(face_speed, 0.0) * (left_value + 0.5 * (1.0 - face_speed) * left_slope)
        flux = flux + jnp.minimum(face_speed, 0.0) * (right_value - 0.5 * (1.0 + face_speed) * right_slope)
        change = change + lax.slice_in_dim(flux, 1, length - 3, axis=cut_dim) - lax.slice_in_dim(flux, 0, length - 4, axis=cut_dim)
    return inner_slice(scalars, 3, 0, 0) - change


def momentum(flow_ext, pressure_ext, wet_ext):
    wet_mid = wet_ext[2:-2]
    height = wet_mid.shape[1] - 4
    breadth = wet_mid.shape[2] - 4

    def neighbour(values, shift_y, shift_x):
        return values[:, 2 + shift_y:2 + shift_y + height, 2 + shift_x:2 + shift_x + breadth]

    offsets = ((0, 1), (0, -1), (1, 0), (-1, 0))
    wet_here = neighbour(wet_mid, 0, 0)
    press_here = neighbour(pressure_ext, 0, 0)
    near_wet = []
    near_press = []
    for number in range(4):
        shift_y, shift_x = offsets[number]
        wet_near = neighbour(wet_mid, shift_y, shift_x)
        near_wet.append(wet_near)
        near_press.append(wet_near * neighbour(pressure_ext, shift_y, shift_x) + (1.0 - wet_near) * press_here)
    grad_x = 0.5 * (near_press[0] - near_press[1])
    grad_y = 0.5 * (near_press[2] - near_press[3])

    def laplace(values):
        total_near = 0.0
        for number in range(4):
            shift_y, shift_x = offsets[number]
            total_near = total_near + near_wet[number] * neighbour(values, shift_y, shift_x)
        return total_near - 4.0 * neighbour(values, 0, 0)

    east_west = flow_ext[0, 2:-2]
    north_south = flow_ext[1, 2:-2]
    zonal = neighbour(east_west, 0, 0)
    meridional = neighbour(north_south, 0, 0)
    zonal_next = wet_here * (zonal + time_step * (coriolis * meridional - grad_x) + viscosity * laplace(east_west))
    merid_next = wet_here * (meridional + time_step * (-coriolis * zonal - grad_y) + viscosity * laplace(north_south))
    return jnp.stack([zonal_next, merid_next], 0)


def light(attenuation, above):
    optical = above + jnp.cumsum(attenuation, 0) - attenuation
    incoming_solar_flux = jnp.exp(-optical)
    return incoming_solar_flux, incoming_solar_flux * (1.0 - jnp.exp(-attenuation))


def drifter_concentration_vector(carried_quantities, incoming_solar_flux, seawater_heat_degrees, marine_point_flag):
    nutrient, phyto, zooplankton, detritus = carried_quantities[0], carried_quantities[1], carried_quantities[2], carried_quantities[3]
    biomass_increase = highest_division_speed * jnp.exp(thermal_multiplier * seawater_heat_degrees) * incoming_solar_flux / (photic_halfway_level + incoming_solar_flux)
    scale_now = bio_step * marine_point_flag
    for substep in range(SUBSTEPS):
        uptake = biomass_increase * nutrient / (half_nutrient + jnp.abs(nutrient)) * phyto
        grazing = zooplankton * phyto * phyto / (half_prey + phyto * phyto)
        nutrient_next = nutrient + scale_now * (remin_rate * detritus - uptake)
        phyto_next = phyto + scale_now * (uptake - grazing - phyto_loss * phyto)
        zoo_next = zooplankton + scale_now * (graze_yield * grazing - zoo_loss * zooplankton)
        detritus = detritus + scale_now * ((1.0 - graze_yield) * grazing + phyto_loss * phyto + zoo_loss * zooplankton - remin_rate * detritus)
        nutrient, phyto, zooplankton = nutrient_next, phyto_next, zoo_next
    return jnp.stack([nutrient, phyto, zooplankton, detritus], 0)


def extend(values, signs):
    folded = jnp.flip(values[:, :, -2:, :], (2, 3)) * signs[:, None, None, None]
    padded = jnp.concatenate([jnp.zeros_like(values[:, :, :2, :]), values, folded], axis=2)
    padded = jnp.concatenate([padded[..., -2:], padded, padded[..., :2]], axis=3)
    zeros_rim = jnp.zeros_like(padded[:, :2])
    return jnp.concatenate([zeros_rim, padded, zeros_rim], axis=1)


def reference(tracers, flow, temp_salt, wet):
    marine_point_flag = wet.astype(jnp.float32)
    one_sign = jnp.ones((1,), jnp.float32)
    flow_ext = extend(flow, jnp.array([-1.0, -1.0, 1.0], jnp.float32))
    wet_ext = extend(marine_point_flag[None], one_sign)[0]

    def advect_one(scalar):
        return advect(extend(scalar[None], one_sign), flow_ext, wet_ext)[0]

    moved_tracers = lax.map(advect_one, tracers)
    moved_heat = lax.map(advect_one, temp_salt)
    density = marine_point_flag * (rho_temp * temp_salt[0] + rho_salt * temp_salt[1])
    pressure = jnp.cumsum(density, 0) - 0.5 * density
    pressure_ext = extend(pressure[None], one_sign)[0, 2:-2]
    flow_next = momentum(flow_ext, pressure_ext, wet_ext)
    attenuation = marine_point_flag * (light_water + light_chloro * tracers[1])
    incoming_solar_flux, absorbed = light(attenuation, 0.0)
    biology = drifter_concentration_vector(moved_tracers, incoming_solar_flux, temp_salt[0], marine_point_flag)
    tracers_next = jnp.concatenate([biology, moved_tracers[4:]], 0)
    temp_salt_next = jnp.stack([moved_heat[0] + heat_gain * absorbed, moved_heat[1]], 0)
    return tracers_next, temp_salt_next, flow_next
```

```python
import functools

import jax
import jax.numpy as jnp
from jax import lax
from jax.experimental import pallas as pl
from jax.experimental.pallas import tpu as pltpu
from jax.sharding import PartitionSpec as P

SUBSTEPS = 4
light_water = 0.04
light_chloro = 0.06
rho_temp = -0.2
rho_salt = 0.8
time_step = 0.02
coriolis = 0.4
viscosity = 0.1
heat_gain = 4.0
photic_halfway_level = 0.2
highest_division_speed = 1.5
half_nutrient = 0.5
half_prey = 0.3
phyto_loss = 0.05
zoo_loss = 0.1
graze_yield = 0.3
remin_rate = 0.15
bio_step = 0.25
thermal_multiplier = 0.063

LANES = 128
PAD = 8


def chunk_list(tracers):
    bounds = [0, 4]
    step = 3
    while bounds[-1] < tracers:
        left = tracers - bounds[-1]
        bounds.append(bounds[-1] + (step if left > step else max(1, left - 1)))
    return list(zip(bounds[:-1], bounds[1:]))


def minmod(former, latter):
    return jnp.maximum(
        jnp.minimum(former, latter), jnp.minimum(jnp.maximum(former, latter), 0.0)
    )


def face_terms(speed):
    return jnp.where(speed > 0.0, 0.5 * (1.0 - speed), -0.5 * (1.0 + speed))


def upwind(speed, weight, low, high, low_slope, high_slope):
    forward = speed > 0.0
    value = jnp.where(forward, low, high)
    slope = jnp.where(forward, low_slope, high_slope)
    return speed * (value + weight * slope)


def running_sum(values, stride):
    rows = values.shape[0]
    index = lax.broadcasted_iota(jnp.int32, values.shape, 0)
    shift = stride
    while shift < rows:
        moved = pltpu.roll(values, shift, 0)
        values = values + jnp.where(index >= shift, moved, 0.0)
        shift *= 2
    return values


def kernel(
    tr,
    fl,
    ts,
    wt,
    otr,
    ots,
    ofl,
    q,
    flow,
    wet_raw,
    wet,
    acc,
    mom,
    halo,
    edge_out,
    edge,
    pack,
    pack_in,
    line,
    side,
    cz,
    hz,
    cx,
    hx,
    cy,
    hy,
    growth,
    absorbed,
    fz,
    sz,
    nbr,
    load_sem,
    pack_send,
    pack_recv,
    send_sem,
    recv_sem,
    store_sem,
):
    tracers = tr.shape[0]
    fields = tracers + 2
    rows = q.shape[1] - 2 * PAD
    levels = rows // 2
    temp, salt = tracers, tracers + 1
    chunks = chunk_list(tracers)
    whole = slice(PAD, PAD + rows)

    grp, gx, gy = lax.axis_index("grp"), lax.axis_index("gx"), lax.axis_index("gy")
    n_grp, n_gx, n_gy = lax.axis_size("grp"), lax.axis_size("gx"), lax.axis_size("gy")
    lon, n_lon = grp * n_gx + gx, n_grp * n_gx
    right_lon = (lon + 1) % n_lon
    left_lon = (lon + n_lon - 1) % n_lon
    right = (right_lon // n_gx, right_lon % n_gx, gy)
    left = (left_lon // n_gx, left_lon % n_gx, gy)
    top = (gy + 1) // n_gy
    is_top = gy == n_gy - 1
    has_south = gy > 0
    north = (
        grp + top * (n_grp - 1 - 2 * grp),
        gx + top * (n_gx - 1 - 2 * gx),
        gy + 1 - top,
    )
    south = (grp, gx, jnp.maximum(gy - 1, 0))
    mesh_id = pl.DeviceIdType.MESH

    barrier = pltpu.get_barrier_semaphore()
    for other in (north, left, right):
        pl.semaphore_signal(barrier, inc=1, device_id=other, device_id_type=mesh_id)

    @pl.when(has_south)
    def _():
        pl.semaphore_signal(barrier, inc=1, device_id=south, device_id_type=mesh_id)

    loads = [
        pltpu.make_async_copy(wt, wet_raw, load_sem.at[0]),
        pltpu.make_async_copy(fl, flow.at[:, whole], load_sem.at[1]),
        pltpu.make_async_copy(ts, q.at[tracers:fields, whole], load_sem.at[2]),
        pltpu.make_async_copy(tr, q.at[0:tracers, whole], load_sem.at[3]),
    ]
    for load in loads:
        load.start()

    zeros = jnp.zeros((PAD, LANES), jnp.float32)
    below = slice(PAD + rows, PAD + rows + PAD)
    for pads in (wet, flow.at[0], fz, sz):
        pads[0:PAD] = zeros
        pads[below] = zeros

    @pl.loop(0, fields)
    def _(f):
        q[f, 0:PAD] = zeros
        q[f, below] = zeros

    lane = lax.broadcasted_iota(jnp.int32, (rows, LANES), 1)
    quad = lane // 4
    spot = lane % 4
    first, last = lane == 0, lane == LANES - 1

    def row_of(ref, r):
        return ref[pl.ds(r, levels, stride=2), :]

    loads[0].wait()
    wet[whole] = wet_raw[...].astype(jnp.float32)
    loads[1].wait()
    for way, r in ((0, 1), (1, 0)):
        for slot in range(2):
            edge_out[way, slot] = flow[slot, pl.ds(PAD + r, levels, stride=2), :]
        edge_out[way, 2] = wet[pl.ds(PAD + r, levels, stride=2), :]
    loads[2].wait()
    loads[3].wait()

    def take(f, packed):
        turned = pltpu.roll(q[f, whole], 4 * f + 2, 1)
        return jnp.where(quad == f, turned, packed)

    packed = lax.fori_loop(0, fields, take, jnp.zeros((rows, LANES), jnp.float32))
    for slot in range(3):
        f = fields + slot
        packed = jnp.where(quad == f, pltpu.roll(flow[slot, whole], 4 * f + 2, 1), packed)
    f = fields + 3
    packed = jnp.where(quad == f, pltpu.roll(wet[whole], 4 * f + 2, 1), packed)
    pack[...] = packed

    @pl.when(has_south)
    def _():
        pl.semaphore_wait(barrier, 4)

    @pl.when(jnp.logical_not(has_south))
    def _():
        pl.semaphore_wait(barrier, 3)

    to_right = pltpu.make_async_remote_copy(
        pack, pack_in.at[0], pack_send.at[0], pack_recv.at[0], right, mesh_id
    )
    to_left = pltpu.make_async_remote_copy(
        pack, pack_in.at[1], pack_send.at[1], pack_recv.at[1], left, mesh_id
    )
    to_right.start()
    to_left.start()

    def piece(number, way, slot, device):
        if number == 0:
            source, target = edge_out.at[way], edge.at[slot]
        elif number == 1:
            source, target = ts, halo.at[slot, tracers:fields]
        else:
            lo, hi = chunks[number - 2]
            source, target = tr.at[lo:hi], halo.at[slot, lo:hi]
        return pltpu.make_async_remote_copy(
            source,
            target,
            send_sem.at[way, number],
            recv_sem.at[slot, number],
            device,
            mesh_id,
        )

    pieces = len(chunks) + 2
    for number in range(pieces):
        piece(number, 0, top, north).start()

        @pl.when(has_south)
        def _():
            piece(number, 1, 1, south).start()

    @pl.when(jnp.logical_not(has_south))
    def _():
        edge[0] = jnp.zeros((3, levels, LANES), jnp.float32)

        @pl.loop(0, fields)
        def _(f):
            halo[0, f] = jnp.zeros((rows, LANES), jnp.float32)

    mirror = LANES - 1 - lax.broadcasted_iota(jnp.int32, (levels, LANES), 1)

    def flip(values):
        return jnp.take_along_axis(values, mirror, axis=1)

    def await_piece(number):
        @pl.when(has_south)
        def _():
            piece(number, 0, 0, south).wait_recv()

        piece(number, 1, 1, south).wait_recv()

        @pl.when(is_top)
        def _():
            if number == 0:
                edge[1, 0] = -flip(edge[1, 0])
                edge[1, 1] = -flip(edge[1, 1])
                edge[1, 2] = flip(edge[1, 2])
            else:
                lo, hi = (tracers, fields) if number == 1 else chunks[number - 2]

                @pl.loop(lo, hi)
                def _(f):
                    here = halo.at[1, f]
                    near, far = flip(row_of(here, 1)), flip(row_of(here, 0))
                    here[pl.ds(0, levels, stride=2), :] = near
                    here[pl.ds(1, levels, stride=2), :] = far

    wet_here = wet[whole]

    speed = 0.5 * (flow[0, whole] + flow[0, PAD + 2 : PAD + 2 + rows])
    speed = speed * wet_here * wet[PAD + 2 : PAD + 2 + rows]
    cz[...] = speed
    hz[...] = face_terms(speed)

    attenuation = wet_here * (light_water + light_chloro * q[1, whole])
    light_top = jnp.exp(-(running_sum(attenuation, 2) - attenuation))
    absorbed[...] = light_top * (1.0 - jnp.exp(-attenuation))
    growth[...] = (
        highest_division_speed
        * jnp.exp(thermal_multiplier * q[temp, whole])
        * light_top
        / (photic_halfway_level + light_top)
    )

    to_right.wait_recv()
    to_left.wait_recv()
    own = pack[...]
    lines = jnp.where(spot < 2, pack_in[0], pack_in[1])
    line[...] = lines

    def beyond(ref, f):
        return pltpu.roll(ref[...], LANES - 2 - 4 * f, 1)

    def east(values, outer):
        return pltpu.roll(jnp.where(first, outer, values), LANES - 1, 1)

    def west(values, outer):
        return pltpu.roll(jnp.where(last, outer, values), 1, 1)

    eastward = flow[2, whole]
    outer_wet = beyond(line, fields + 3)
    outer_flow = beyond(line, fields + 2)
    wet_east, wet_west = east(wet_here, outer_wet), west(wet_here, outer_wet)
    speed = 0.5 * (eastward + east(eastward, outer_flow)) * wet_here * wet_east
    cx[...] = speed
    hx[...] = face_terms(speed)
    entry = 0.5 * (west(eastward, outer_flow) + eastward) * wet_west * wet_here
    entry = jnp.broadcast_to(entry[:, 0:1], (rows, LANES))

    low_line = jnp.where(spot < 2, lines, own)
    low_next = pltpu.roll(low_line, LANES - 1, 1)
    gap = low_next - low_line
    low_slope = minmod(gap, pltpu.roll(gap, 1, 1))
    entry_flux = upwind(
        entry,
        face_terms(entry),
        low_line,
        low_next,
        low_slope,
        pltpu.roll(low_slope, LANES - 1, 1),
    )
    high_line = jnp.where(spot < 2, own, lines)
    gap = pltpu.roll(high_line, LANES - 1, 1) - high_line
    high_slope = minmod(gap, pltpu.roll(gap, 1, 1))
    side[...] = jnp.where(spot == 1, entry_flux, high_slope)

    @pl.loop(0, fields)
    def _(f):
        here = q[f, whole]
        deeper, higher = q[f, PAD + 2 : PAD + 2 + rows], q[f, PAD - 2 : PAD - 2 + rows]
        slope = minmod(deeper - here, here - higher)
        sz[whole] = slope
        flux = upwind(
            cz[...], hz[...], here, deeper, slope, sz[PAD + 2 : PAD + 2 + rows]
        )
        fz[whole] = flux
        change = flux - fz[PAD - 2 : PAD - 2 + rows]
        outer, outer_side = beyond(line, f), beyond(side, f)
        next_east = east(here, outer)
        slope = minmod(next_east - here, here - west(here, outer))
        flux = upwind(
            cx[...], hx[...], here, next_east, slope, east(slope, outer_side)
        )
        acc[f] = here - (change + (flux - west(flux, outer_side)))

    await_piece(0)
    own_rows = [wet[pl.ds(PAD + r, levels, stride=2), :] for r in range(2)]
    wets = [edge[0, 2]] + own_rows + [edge[1, 2]]
    flows = [edge[0, 1]]
    flows += [flow[1, pl.ds(PAD + r, levels, stride=2), :] for r in range(2)]
    flows += [edge[1, 1]]
    for face in range(3):
        speed = 0.5 * (flows[face] + flows[face + 1]) * wets[face] * wets[face + 1]
        cy[face] = speed
        hy[face] = face_terms(speed)

    def across(f):
        for block in range(levels // 8):
            span = slice(8 * block, 8 * block + 8)

            def load(ref, start, r):
                return ref[pl.ds(start + 16 * block + r, 8, stride=2), :]

            here = q.at[f]
            values = [load(halo.at[0, f], 0, 0), load(halo.at[0, f], 0, 1)]
            values += [load(here, PAD, 0), load(here, PAD, 1)]
            values += [load(halo.at[1, f], 0, 0), load(halo.at[1, f], 0, 1)]
            gaps = [values[i + 1] - values[i] for i in range(5)]
            slopes = [minmod(gaps[i + 1], gaps[i]) for i in range(4)]
            fluxes = [
                upwind(
                    cy[i, span],
                    hy[i, span],
                    values[i + 1],
                    values[i + 2],
                    slopes[i],
                    slopes[i + 1],
                )
                for i in range(3)
            ]
            for r in range(2):
                target = (f, pl.ds(16 * block + r, 8, stride=2), slice(None))
                acc[target] = acc[target] - (fluxes[r + 1] - fluxes[r])

    await_piece(1)

    @pl.loop(tracers, fields)
    def _(f):
        across(f)

    acc[temp] = acc[temp] + heat_gain * absorbed[...]
    out_ts = pltpu.make_async_copy(acc.at[tracers:fields], ots, store_sem.at[0])
    out_ts.start()

    def weigh(wetness, heat, salinity):
        return wetness * (rho_temp * heat + rho_salt * salinity)

    def pressure_of(density, stride):
        return running_sum(density, stride) - 0.5 * density

    press = pressure_of(weigh(wet_here, q[temp, whole], q[salt, whole]), 2)
    outer_press = pressure_of(weigh(outer_wet, beyond(line, temp), beyond(line, salt)), 2)
    press_south = pressure_of(
        weigh(edge[0, 2], row_of(halo.at[0, temp], 1), row_of(halo.at[0, salt], 1)), 1
    )
    press_north = pressure_of(
        weigh(edge[1, 2], row_of(halo.at[1, temp], 0), row_of(halo.at[1, salt], 0)), 1
    )
    nbr[2] = press

    def spread(slot, own_ref, start, lower, upper):
        nbr[0, pl.ds(0, levels, stride=2), :] = lower
        nbr[0, pl.ds(1, levels, stride=2), :] = own_ref[pl.ds(start, levels, stride=2), :]
        nbr[1, pl.ds(0, levels, stride=2), :] = own_ref[pl.ds(start + 1, levels, stride=2), :]
        nbr[1, pl.ds(1, levels, stride=2), :] = upper
        return nbr[1], nbr[0]

    wet_north, wet_south = spread(0, wet, PAD, edge[0, 2], edge[1, 2])
    near_wet = (wet_east, wet_west, wet_north, wet_south)
    press_n, press_s = spread(1, nbr.at[2], 0, press_south, press_north)
    near = (east(press, outer_press), west(press, outer_press), press_n, press_s)
    near = [w * p + (1.0 - w) * press for w, p in zip(near_wet, near)]
    grad_x = 0.5 * (near[0] - near[1])
    grad_y = 0.5 * (near[2] - near[3])

    def laplace(slot):
        values = flow[slot, whole]
        outer = beyond(line, fields + slot)
        up, down = spread(slot, flow.at[slot], PAD, edge[0, slot], edge[1, slot])
        near_values = (east(values, outer), west(values, outer), up, down)
        total = near_wet[0] * near_values[0]
        for w, value in zip(near_wet[1:], near_values[1:]):
            total = total + w * value
        return total - 4.0 * values

    zonal, merid = flow[0, whole], flow[1, whole]
    mom[0] = wet_here * (
        zonal + time_step * (coriolis * merid - grad_x) + viscosity * laplace(0)
    )
    mom[1] = wet_here * (
        merid + time_step * (-coriolis * zonal - grad_y) + viscosity * laplace(1)
    )
    out_fl = pltpu.make_async_copy(mom, ofl, store_sem.at[1])
    out_fl.start()

    outs = [out_ts, out_fl]
    for number, (lo, hi) in enumerate(chunks):
        await_piece(number + 2)

        @pl.loop(lo, hi)
        def _(f):
            across(f)

        if number == 0:

            @pl.loop(0, rows // 8)
            def _(block):
                span = pl.ds(pl.multiple_of(8 * block, 8), 8)
                wet_span = pl.ds(pl.multiple_of(8 * block + PAD, 8), 8)
                nutrient, phyto, zoo, detritus = [acc[i, span] for i in range(4)]
                speed = growth[span]
                step = bio_step * wet[wet_span]
                for _ in range(SUBSTEPS):
                    uptake = speed * nutrient / (half_nutrient + jnp.abs(nutrient)) * phyto
                    square = phyto * phyto
                    grazing = zoo * square / (half_prey + square)
                    nutrient_next = nutrient + step * (remin_rate * detritus - uptake)
                    phyto_next = phyto + step * (uptake - grazing - phyto_loss * phyto)
                    zoo_next = zoo + step * (graze_yield * grazing - zoo_loss * zoo)
                    detritus = detritus + step * (
                        (1.0 - graze_yield) * grazing
                        + phyto_loss * phyto
                        + zoo_loss * zoo
                        - remin_rate * detritus
                    )
                    nutrient, phyto, zoo = nutrient_next, phyto_next, zoo_next
                for i, value in enumerate((nutrient, phyto, zoo, detritus)):
                    acc[i, span] = value

        out = pltpu.make_async_copy(acc.at[lo:hi], otr.at[lo:hi], store_sem.at[number + 2])
        out.start()
        outs.append(out)

    to_right.wait_send()
    to_left.wait_send()
    for number in range(pieces):
        piece(number, 0, top, north).wait_send()

        @pl.when(has_south)
        def _():
            piece(number, 1, 1, south).wait_send()

    for out in outs:
        out.wait()


def body(tracers, flow, temp_salt, wet):
    count, levels, height, breadth = tracers.shape
    rows = levels * height
    fields = count + 2
    pieces = len(chunk_list(count)) + 2
    f32 = jnp.float32
    field = pltpu.VMEM((rows, breadth), f32)
    padded = pltpu.VMEM((rows + 2 * PAD, breadth), f32)
    dma = pltpu.SemaphoreType.DMA
    anywhere = pl.BlockSpec(memory_space=pl.ANY)
    outs = pl.pallas_call(
        kernel,
        out_shape=(
            jax.ShapeDtypeStruct((count, rows, breadth), f32),
            jax.ShapeDtypeStruct((2, rows, breadth), f32),
            jax.ShapeDtypeStruct((2, rows, breadth), f32),
        ),
        in_specs=[anywhere] * 4,
        out_specs=(anywhere,) * 3,
        scratch_shapes=[
            pltpu.VMEM((fields, rows + 2 * PAD, breadth), f32),
            pltpu.VMEM((3, rows + 2 * PAD, breadth), f32),
            pltpu.VMEM((rows, breadth), jnp.int32),
            padded,
            pltpu.VMEM((fields, rows, breadth), f32),
            pltpu.VMEM((2, rows, breadth), f32),
            pltpu.VMEM((2, fields, rows, breadth), f32),
            pltpu.VMEM((2, 3, levels, breadth), f32),
            pltpu.VMEM((2, 3, levels, breadth), f32),
            field,
            pltpu.VMEM((2, rows, breadth), f32),
            field,
            field,
            field,
            field,
            field,
            field,
            pltpu.VMEM((3, levels, breadth), f32),
            pltpu.VMEM((3, levels, breadth), f32),
            field,
            field,
            padded,
            padded,
            pltpu.VMEM((3, rows, breadth), f32),
            dma((4,)),
            dma((2,)),
            dma((2,)),
            dma((2, pieces)),
            dma((2, pieces)),
            dma((pieces,)),
        ],
        compiler_params=pltpu.CompilerParams(collective_id=0, has_side_effects=True),
    )(
        tracers.reshape(count, rows, breadth),
        flow.reshape(3, rows, breadth),
        temp_salt.reshape(2, rows, breadth),
        wet.reshape(rows, breadth),
    )
    return tuple(out.reshape(-1, levels, height, breadth) for out in outs)


def solution(mesh):
    four = P(None, None, "gy", ("grp", "gx"))
    return jax.shard_map(
        body,
        mesh=mesh,
        in_specs=(four, four, four, P(None, "gy", ("grp", "gx"))),
        out_specs=(four, four, four),
        check_vma=False,
    )
```

```python
import functools

import jax
import jax.numpy as jnp
from jax import lax
from jax.experimental import pallas as pl
from jax.experimental.pallas import tpu as pltpu
from jax.sharding import PartitionSpec as P

SUBSTEPS = 4
light_water = 0.04
light_chloro = 0.06
rho_temp = -0.2
rho_salt = 0.8
time_step = 0.02
coriolis = 0.4
viscosity = 0.1
heat_gain = 4.0
photic_halfway_level = 0.2
highest_division_speed = 1.5
half_nutrient = 0.5
half_prey = 0.3
phyto_loss = 0.05
zoo_loss = 0.1
graze_yield = 0.3
remin_rate = 0.15
bio_step = 0.25
thermal_multiplier = 0.063

LANES = 128
PAD = 8


EDGE, TEMP_SALT = "edge", "temp_salt"


def piece_list(tracers):
    rest = tracers - 4
    sizes = [3, 2, 3, 2, 3]
    scaled = [max(1, size * rest // 15) for size in sizes]
    bounds = [4]
    for size in scaled + [1] * tracers:
        if bounds[-1] < tracers:
            bounds.append(min(tracers, bounds[-1] + size))
    pieces = [(EDGE, 0, 0, False), (TEMP_SALT, tracers, tracers + 2, False), ("tracers", 0, 4, False)]
    for number, (lo, hi) in enumerate(zip(bounds[:-1], bounds[1:])):
        pieces.append(("tracers", lo, hi, number % 2 == 0))
    return pieces


def minmod(former, latter):
    return jnp.maximum(
        jnp.minimum(former, latter), jnp.minimum(jnp.maximum(former, latter), 0.0)
    )


def face_terms(speed):
    return jnp.where(speed > 0.0, 0.5 * (1.0 - speed), -0.5 * (1.0 + speed))


def upwind(speed, weight, low, high, low_slope, high_slope):
    forward = speed > 0.0
    value = jnp.where(forward, low, high)
    slope = jnp.where(forward, low_slope, high_slope)
    return speed * (value + weight * slope)


def running_sum(values, stride):
    rows = values.shape[0]
    index = lax.broadcasted_iota(jnp.int32, values.shape, 0)
    shift = stride
    while shift < rows:
        moved = pltpu.roll(values, shift, 0)
        values = values + jnp.where(index >= shift, moved, 0.0)
        shift *= 2
    return values


def kernel(
    tr,
    fl,
    ts,
    wt,
    acc,
    heat,
    mom,
    q,
    flow,
    wet_raw,
    wet,
    halo,
    edge_out,
    edge,
    pack,
    pack_in,
    line,
    side,
    cz,
    hz,
    cx,
    hx,
    cy,
    hy,
    growth,
    absorbed,
    fz,
    sz,
    nbr,
    transit,
    load_sem,
    pack_send,
    pack_recv,
    send_sem,
    recv_sem,
    relay_send,
    relay_recv,
):
    tracers = tr.shape[0]
    fields = tracers + 2
    rows = q.shape[1] - 2 * PAD
    levels = rows // 2
    temp, salt = tracers, tracers + 1
    pieces = piece_list(tracers)
    whole = slice(PAD, PAD + rows)

    grp, gx, gy = lax.axis_index("grp"), lax.axis_index("gx"), lax.axis_index("gy")
    n_grp, n_gx, n_gy = lax.axis_size("grp"), lax.axis_size("gx"), lax.axis_size("gy")
    lon, n_lon = grp * n_gx + gx, n_grp * n_gx

    def place(index):
        return index // n_gx, index % n_gx

    def depth(index):
        return (index % n_gx) // (n_gx // 2) * n_grp + index // n_gx

    right_lon = (lon + 1) % n_lon
    left_lon = (lon + n_lon - 1) % n_lon
    mirror_lon = n_lon - 1 - lon
    right, left = (*place(right_lon), gy), (*place(left_lon), gy)
    north, south = (grp, gx, jnp.minimum(gy + 1, n_gy - 1)), (grp, gx, jnp.maximum(gy - 1, 0))
    partner = (*place(mirror_lon), n_gy - 1)
    carrier = (*place(mirror_lon), 0)
    own_top, own_bottom = (grp, gx, n_gy - 1), (grp, gx, 0)
    is_top, has_south = gy == n_gy - 1, gy > 0
    has_north = gy < n_gy - 1
    here, over_right, over_left = depth(lon), depth(right_lon), depth(left_lon)
    early_right, early_left = here < over_right, here < over_left
    late_right, late_left = here > over_right, here > over_left
    early_fold = here < depth(mirror_lon)
    answers = is_top & early_fold
    opens = is_top & jnp.logical_not(early_fold)
    relays = (gy == 0) & early_fold
    waits_east_west = early_right | early_left
    mesh_id = pl.DeviceIdType.MESH

    barrier = pltpu.get_barrier_semaphore()

    def greet(condition, other):
        @pl.when(condition)
        def _():
            pl.semaphore_signal(barrier, inc=1, device_id=other, device_id_type=mesh_id)

    greet(answers, partner)
    greet(relays, partner)
    greet(answers, own_bottom)
    greet(has_north, north)
    greet(has_south, south)
    greet(jnp.logical_not(late_right), right)
    greet(jnp.logical_not(late_left), left)

    def one(condition):
        return jnp.where(condition, 1, 0)

    expected = one(has_north) + one(has_south) + one(opens) * 2 + one(relays)
    expected += one(jnp.logical_not(early_right)) + one(jnp.logical_not(early_left))

    loads = [
        pltpu.make_async_copy(wt, wet_raw, load_sem.at[0]),
        pltpu.make_async_copy(fl, flow.at[:, whole], load_sem.at[1]),
        pltpu.make_async_copy(ts, q.at[tracers:fields, whole], load_sem.at[2]),
        pltpu.make_async_copy(tr, q.at[0:tracers, whole], load_sem.at[3]),
    ]
    for load in loads:
        load.start()

    def piece(number, way, slot, device):
        kind, lo, hi, _ = pieces[number]
        if kind == EDGE:
            source, target = edge_out.at[way], edge.at[slot]
        elif kind == TEMP_SALT:
            source, target = ts, halo.at[slot, lo:hi]
        else:
            source, target = tr.at[lo:hi], halo.at[slot, lo:hi]
        return pltpu.make_async_remote_copy(
            source,
            target,
            send_sem.at[way, number],
            recv_sem.at[slot, number],
            device,
            mesh_id,
        )

    relayed = [number for number, entry in enumerate(pieces) if entry[3]]
    berth, total = {}, 0
    for number in relayed:
        berth[number] = total
        total += pieces[number][2] - pieces[number][1]

    def to_carrier(number):
        _, lo, hi, _ = pieces[number]
        start = berth[number]
        return pltpu.make_async_remote_copy(
            tr.at[lo:hi],
            transit.at[start : start + hi - lo],
            send_sem.at[0, number],
            relay_recv.at[number],
            carrier,
            mesh_id,
        )

    def from_carrier(number):
        _, lo, hi, _ = pieces[number]
        start = berth[number]
        return pltpu.make_async_remote_copy(
            transit.at[start : start + hi - lo],
            halo.at[1, lo:hi],
            relay_send.at[number],
            recv_sem.at[1, number],
            own_top,
            mesh_id,
        )

    def send(number):
        @pl.when(opens)
        def _():
            if number in berth:
                to_carrier(number).start()
            else:
                piece(number, 0, 1, partner).start()

        @pl.when(has_north)
        def _():
            piece(number, 0, 0, north).start()

        @pl.when(has_south)
        def _():
            piece(number, 1, 1, south).start()

    pl.semaphore_wait(barrier, expected)
    send(1)

    loads[0].wait()
    wet[whole] = wet_raw[...].astype(jnp.float32)
    loads[1].wait()
    for way, r in ((0, 1), (1, 0)):
        for slot in range(2):
            edge_out[way, slot] = flow[slot, pl.ds(PAD + r, levels, stride=2), :]
        edge_out[way, 2] = wet[pl.ds(PAD + r, levels, stride=2), :]

    zeros = jnp.zeros((PAD, LANES), jnp.float32)
    below = slice(PAD + rows, PAD + rows + PAD)
    for pads in (wet, flow.at[0], fz, sz):
        pads[0:PAD] = zeros
        pads[below] = zeros

    @pl.loop(0, fields)
    def _(f):
        q[f, 0:PAD] = zeros
        q[f, below] = zeros

    for number in (0, *range(2, len(pieces))):
        send(number)

    lane = lax.broadcasted_iota(jnp.int32, (rows, LANES), 1)
    quad = lane // 4
    spot = lane % 4
    first, last = lane == 0, lane == LANES - 1

    def row_of(ref, r):
        return ref[pl.ds(r, levels, stride=2), :]

    loads[2].wait()
    loads[3].wait()

    def take(f, packed):
        turned = pltpu.roll(q[f, whole], 4 * f + 2, 1)
        return jnp.where(quad == f, turned, packed)

    packed = lax.fori_loop(0, fields, take, jnp.zeros((rows, LANES), jnp.float32))
    for slot in range(3):
        f = fields + slot
        packed = jnp.where(quad == f, pltpu.roll(flow[slot, whole], 4 * f + 2, 1), packed)
    f = fields + 3
    packed = jnp.where(quad == f, pltpu.roll(wet[whole], 4 * f + 2, 1), packed)
    pack[...] = packed

    @pl.when(jnp.logical_not(has_south))
    def _():
        edge[0] = jnp.zeros((3, levels, LANES), jnp.float32)

        @pl.loop(0, fields)
        def _(f):
            halo[0, f] = jnp.zeros((rows, LANES), jnp.float32)

    mirror = LANES - 1 - lax.broadcasted_iota(jnp.int32, (levels, LANES), 1)

    def flip(values):
        return jnp.take_along_axis(values, mirror, axis=1)

    def await_piece(number):
        kind, lo, hi, _ = pieces[number]

        @pl.when(has_south)
        def _():
            piece(number, 0, 0, south).wait_recv()

        piece(number, 1, 1, south).wait_recv()
        if number == 0:

            @pl.when(answers)
            def _():
                for other in range(len(pieces)):
                    piece(other, 0, 1, partner).start()

        @pl.when(is_top)
        def _():
            if kind == EDGE:
                edge[1, 0] = -flip(edge[1, 0])
                edge[1, 1] = -flip(edge[1, 1])
                edge[1, 2] = flip(edge[1, 2])
            else:

                @pl.loop(lo, hi)
                def _(f):
                    there = halo.at[1, f]
                    near, far = flip(row_of(there, 1)), flip(row_of(there, 0))
                    there[pl.ds(0, levels, stride=2), :] = near
                    there[pl.ds(1, levels, stride=2), :] = far

    wet_here = wet[whole]

    speed = 0.5 * (flow[0, whole] + flow[0, PAD + 2 : PAD + 2 + rows])
    speed = speed * wet_here * wet[PAD + 2 : PAD + 2 + rows]
    cz[...] = speed
    hz[...] = face_terms(speed)

    attenuation = wet_here * (light_water + light_chloro * q[1, whole])
    light_top = jnp.exp(-(running_sum(attenuation, 2) - attenuation))
    absorbed[...] = light_top * (1.0 - jnp.exp(-attenuation))
    growth[...] = (
        highest_division_speed
        * jnp.exp(thermal_multiplier * q[temp, whole])
        * light_top
        / (photic_halfway_level + light_top)
    )

    to_right = pltpu.make_async_remote_copy(
        pack, pack_in.at[0], pack_send.at[0], pack_recv.at[0], right, mesh_id
    )
    to_left = pltpu.make_async_remote_copy(
        pack, pack_in.at[1], pack_send.at[1], pack_recv.at[1], left, mesh_id
    )

    @pl.when(jnp.logical_not(early_right))
    def _():
        to_right.start()

    @pl.when(jnp.logical_not(early_left))
    def _():
        to_left.start()

    def beyond(ref, f):
        return pltpu.roll(ref[...], LANES - 2 - 4 * f, 1)

    def east(values, outer):
        return pltpu.roll(jnp.where(first, outer, values), LANES - 1, 1)

    def west(values, outer):
        return pltpu.roll(jnp.where(last, outer, values), 1, 1)

    @pl.loop(0, fields)
    def _(f):
        here = q[f, whole]
        deeper, higher = q[f, PAD + 2 : PAD + 2 + rows], q[f, PAD - 2 : PAD - 2 + rows]
        slope = minmod(deeper - here, here - higher)
        sz[whole] = slope
        flux = upwind(
            cz[...], hz[...], here, deeper, slope, sz[PAD + 2 : PAD + 2 + rows]
        )
        fz[whole] = flux
        acc[f] = here - (flux - fz[PAD - 2 : PAD - 2 + rows])

    def along_longitude():
        to_right.wait_recv()
        to_left.wait_recv()

        @pl.when(early_right)
        def _():
            to_right.start()

        @pl.when(early_left)
        def _():
            to_left.start()

        own = pack[...]
        lines = jnp.where(spot < 2, pack_in[0], pack_in[1])
        line[...] = lines
        wet_here = wet[whole]
        eastward = flow[2, whole]
        outer_wet = beyond(line, fields + 3)
        outer_flow = beyond(line, fields + 2)
        wet_east, wet_west = east(wet_here, outer_wet), west(wet_here, outer_wet)
        speed = 0.5 * (eastward + east(eastward, outer_flow)) * wet_here * wet_east
        cx[...] = speed
        hx[...] = face_terms(speed)
        entry = 0.5 * (west(eastward, outer_flow) + eastward) * wet_west * wet_here
        entry = jnp.broadcast_to(entry[:, 0:1], (rows, LANES))

        low_line = jnp.where(spot < 2, lines, own)
        low_next = pltpu.roll(low_line, LANES - 1, 1)
        gap = low_next - low_line
        low_slope = minmod(gap, pltpu.roll(gap, 1, 1))
        entry_flux = upwind(
            entry,
            face_terms(entry),
            low_line,
            low_next,
            low_slope,
            pltpu.roll(low_slope, LANES - 1, 1),
        )
        high_line = jnp.where(spot < 2, own, lines)
        gap = pltpu.roll(high_line, LANES - 1, 1) - high_line
        high_slope = minmod(gap, pltpu.roll(gap, 1, 1))
        side[...] = jnp.where(spot == 1, entry_flux, high_slope)

        @pl.loop(0, fields)
        def _(f):
            here = q[f, whole]
            outer, outer_side = beyond(line, f), beyond(side, f)
            next_east = east(here, outer)
            slope = minmod(next_east - here, here - west(here, outer))
            flux = upwind(
                cx[...], hx[...], here, next_east, slope, east(slope, outer_side)
            )
            acc[f] = acc[f] - (flux - west(flux, outer_side))

    @pl.when(jnp.logical_not(waits_east_west))
    def _():
        along_longitude()

    await_piece(0)
    own_rows = [wet[pl.ds(PAD + r, levels, stride=2), :] for r in range(2)]
    wets = [edge[0, 2]] + own_rows + [edge[1, 2]]
    flows = [edge[0, 1]]
    flows += [flow[1, pl.ds(PAD + r, levels, stride=2), :] for r in range(2)]
    flows += [edge[1, 1]]
    for face in range(3):
        speed = 0.5 * (flows[face] + flows[face + 1]) * wets[face] * wets[face + 1]
        cy[face] = speed
        hy[face] = face_terms(speed)

    def across(f):
        for block in range(levels // 8):
            span = slice(8 * block, 8 * block + 8)

            def load(ref, start, r):
                return ref[pl.ds(start + 16 * block + r, 8, stride=2), :]

            here = q.at[f]
            values = [load(halo.at[0, f], 0, 0), load(halo.at[0, f], 0, 1)]
            values += [load(here, PAD, 0), load(here, PAD, 1)]
            values += [load(halo.at[1, f], 0, 0), load(halo.at[1, f], 0, 1)]
            gaps = [values[i + 1] - values[i] for i in range(5)]
            slopes = [minmod(gaps[i + 1], gaps[i]) for i in range(4)]
            fluxes = [
                upwind(
                    cy[i, span],
                    hy[i, span],
                    values[i + 1],
                    values[i + 2],
                    slopes[i],
                    slopes[i + 1],
                )
                for i in range(3)
            ]
            for r in range(2):
                target = (f, pl.ds(16 * block + r, 8, stride=2), slice(None))
                acc[target] = acc[target] - (fluxes[r + 1] - fluxes[r])

    def rows_of_piece(number):
        await_piece(number)
        _, lo, hi, _ = pieces[number]

        @pl.loop(lo, hi)
        def _(f):
            across(f)

    def finish():
        wet_here = wet[whole]
        outer_wet = beyond(line, fields + 3)
        wet_east, wet_west = east(wet_here, outer_wet), west(wet_here, outer_wet)
        heat[0] = acc[temp] + heat_gain * absorbed[...]
        heat[1] = acc[salt]

        def weigh(wetness, heat, salinity):
            return wetness * (rho_temp * heat + rho_salt * salinity)

        def pressure_of(density, stride):
            return running_sum(density, stride) - 0.5 * density

        press = pressure_of(weigh(wet_here, q[temp, whole], q[salt, whole]), 2)
        outer_press = pressure_of(weigh(outer_wet, beyond(line, temp), beyond(line, salt)), 2)
        press_south = pressure_of(
            weigh(edge[0, 2], row_of(halo.at[0, temp], 1), row_of(halo.at[0, salt], 1)), 1
        )
        press_north = pressure_of(
            weigh(edge[1, 2], row_of(halo.at[1, temp], 0), row_of(halo.at[1, salt], 0)), 1
        )
        nbr[2] = press

        def spread(slot, own_ref, start, lower, upper):
            nbr[0, pl.ds(0, levels, stride=2), :] = lower
            nbr[0, pl.ds(1, levels, stride=2), :] = own_ref[pl.ds(start, levels, stride=2), :]
            nbr[1, pl.ds(0, levels, stride=2), :] = own_ref[pl.ds(start + 1, levels, stride=2), :]
            nbr[1, pl.ds(1, levels, stride=2), :] = upper
            return nbr[1], nbr[0]

        wet_north, wet_south = spread(0, wet, PAD, edge[0, 2], edge[1, 2])
        near_wet = (wet_east, wet_west, wet_north, wet_south)
        press_n, press_s = spread(1, nbr.at[2], 0, press_south, press_north)
        near = (east(press, outer_press), west(press, outer_press), press_n, press_s)
        near = [w * p + (1.0 - w) * press for w, p in zip(near_wet, near)]
        grad_x = 0.5 * (near[0] - near[1])
        grad_y = 0.5 * (near[2] - near[3])

        def laplace(slot):
            values = flow[slot, whole]
            outer = beyond(line, fields + slot)
            up, down = spread(slot, flow.at[slot], PAD, edge[0, slot], edge[1, slot])
            near_values = (east(values, outer), west(values, outer), up, down)
            total = near_wet[0] * near_values[0]
            for w, value in zip(near_wet[1:], near_values[1:]):
                total = total + w * value
            return total - 4.0 * values

        zonal, merid = flow[0, whole], flow[1, whole]
        mom[0] = wet_here * (
            zonal + time_step * (coriolis * merid - grad_x) + viscosity * laplace(0)
        )
        mom[1] = wet_here * (
            merid + time_step * (-coriolis * zonal - grad_y) + viscosity * laplace(1)
        )
        @pl.loop(0, rows // 8)
        def _(block):
            span = pl.ds(pl.multiple_of(8 * block, 8), 8)
            wet_span = pl.ds(pl.multiple_of(8 * block + PAD, 8), 8)
            nutrient, phyto, zoo, detritus = [acc[i, span] for i in range(4)]
            speed = growth[span]
            step = bio_step * wet[wet_span]
            for _ in range(SUBSTEPS):
                uptake = speed * nutrient / (half_nutrient + jnp.abs(nutrient)) * phyto
                square = phyto * phyto
                grazing = zoo * square / (half_prey + square)
                nutrient_next = nutrient + step * (remin_rate * detritus - uptake)
                phyto_next = phyto + step * (uptake - grazing - phyto_loss * phyto)
                zoo_next = zoo + step * (graze_yield * grazing - zoo_loss * zoo)
                detritus = detritus + step * (
                    (1.0 - graze_yield) * grazing
                    + phyto_loss * phyto
                    + zoo_loss * zoo
                    - remin_rate * detritus
                )
                nutrient, phyto, zoo = nutrient_next, phyto_next, zoo_next
            for i, value in enumerate((nutrient, phyto, zoo, detritus)):
                acc[i, span] = value


    for number in (1, 2):
        rows_of_piece(number)

    @pl.when(waits_east_west & is_top)
    def _():
        along_longitude()

    @pl.when(jnp.logical_not(waits_east_west) | is_top)
    def _():
        finish()

    for number in range(3, len(pieces)):
        rows_of_piece(number)

    @pl.when(waits_east_west & has_north)
    def _():
        along_longitude()
        finish()

    @pl.when(relays)
    def _():
        for number in relayed:
            to_carrier(number).wait_recv()
            from_carrier(number).start()
        for number in relayed:
            from_carrier(number).wait_send()

    to_right.wait_send()
    to_left.wait_send()
    for number in range(len(pieces)):
        piece(number, 0, 0, north).wait_send()

        @pl.when(has_south)
        def _():
            piece(number, 1, 1, south).wait_send()


def write_out(acc, heat, mom, otr, ots, ofl, sem):
    outs = [
        pltpu.make_async_copy(acc.at[0 : otr.shape[0]], otr, sem.at[0]),
        pltpu.make_async_copy(heat, ots, sem.at[1]),
        pltpu.make_async_copy(mom, ofl, sem.at[2]),
    ]
    for out in outs:
        out.start()
    for out in outs:
        out.wait()


def body(tracers, flow, temp_salt, wet):
    count, levels, height, breadth = tracers.shape
    rows = levels * height
    fields = count + 2
    entries = piece_list(count)
    pieces = len(entries)
    moored = sum(hi - lo for _, lo, hi, relay in entries if relay)
    f32 = jnp.float32
    field = pltpu.VMEM((rows, breadth), f32)
    padded = pltpu.VMEM((rows + 2 * PAD, breadth), f32)
    dma = pltpu.SemaphoreType.DMA
    anywhere = pl.BlockSpec(memory_space=pl.ANY)
    local = pl.BlockSpec(memory_space=pltpu.VMEM)
    pair = (2, rows, breadth)
    results = pl.pallas_call(
        kernel,
        out_shape=(
            pltpu.VMEM((fields, rows, breadth), f32),
            pltpu.VMEM(pair, f32),
            pltpu.VMEM(pair, f32),
        ),
        in_specs=[anywhere] * 4,
        out_specs=(local,) * 3,
        scratch_shapes=[
            pltpu.VMEM((fields, rows + 2 * PAD, breadth), f32),
            pltpu.VMEM((3, rows + 2 * PAD, breadth), f32),
            pltpu.VMEM((rows, breadth), jnp.int32),
            padded,
            pltpu.VMEM((2, fields, rows, breadth), f32),
            pltpu.VMEM((2, 3, levels, breadth), f32),
            pltpu.VMEM((2, 3, levels, breadth), f32),
            field,
            pltpu.VMEM(pair, f32),
            field,
            field,
            field,
            field,
            field,
            field,
            pltpu.VMEM((3, levels, breadth), f32),
            pltpu.VMEM((3, levels, breadth), f32),
            field,
            field,
            padded,
            padded,
            pltpu.VMEM((3, rows, breadth), f32),
            pltpu.VMEM((max(1, moored), rows, breadth), f32),
            dma((4,)),
            dma((2,)),
            dma((2,)),
            dma((2, pieces)),
            dma((2, pieces)),
            dma((pieces,)),
            dma((pieces,)),
        ],
        compiler_params=pltpu.CompilerParams(collective_id=0, has_side_effects=True),
        name="step",
    )(
        tracers.reshape(count, rows, breadth),
        flow.reshape(3, rows, breadth),
        temp_salt.reshape(2, rows, breadth),
        wet.reshape(rows, breadth),
    )
    outs = pl.pallas_call(
        write_out,
        out_shape=(
            jax.ShapeDtypeStruct((count, rows, breadth), f32),
            jax.ShapeDtypeStruct(pair, f32),
            jax.ShapeDtypeStruct(pair, f32),
        ),
        in_specs=[local] * 3,
        out_specs=(anywhere,) * 3,
        scratch_shapes=[dma((3,))],
        name="write_out",
    )(*(pltpu.with_memory_space_constraint(value, pltpu.VMEM) for value in results))
    return tuple(out.reshape(-1, levels, height, breadth) for out in outs)


def solution(mesh):
    four = P(None, None, "gy", ("grp", "gx"))
    return jax.shard_map(
        body,
        mesh=mesh,
        in_specs=(four, four, four, P(None, "gy", ("grp", "gx"))),
        out_specs=(four, four, four),
        check_vma=False,
    )
```

```python
import functools

import jax
import jax.numpy as jnp
from jax import lax
from jax.experimental import pallas as pl
from jax.experimental.pallas import tpu as pltpu
from jax.sharding import PartitionSpec as P

SUBSTEPS = 4
light_water = 0.04
light_chloro = 0.06
rho_temp = -0.2
rho_salt = 0.8
time_step = 0.02
coriolis = 0.4
viscosity = 0.1
heat_gain = 4.0
photic_halfway_level = 0.2
highest_division_speed = 1.5
half_nutrient = 0.5
half_prey = 0.3
phyto_loss = 0.05
zoo_loss = 0.1
graze_yield = 0.3
remin_rate = 0.15
bio_step = 0.25
thermal_multiplier = 0.063

LANES = 128
PAD = 8


EDGE, TEMP_SALT = "edge", "temp_salt"


def piece_list(tracers):
    pieces = [(EDGE, 0, 0, False), (TEMP_SALT, tracers, tracers + 2, False), ("tracers", 0, 4, False)]
    plan = ((4, True), (2, False), (4, True), (2, False), (2, True), (tracers, True))
    start = 4
    for size, relay in plan:
        stop = min(tracers, start + size)
        if stop > start:
            pieces.append(("tracers", start, stop, relay))
        start = stop
    return pieces


def minmod(former, latter):
    return jnp.maximum(
        jnp.minimum(former, latter), jnp.minimum(jnp.maximum(former, latter), 0.0)
    )


def face_terms(speed):
    return jnp.where(speed > 0.0, 0.5 * (1.0 - speed), -0.5 * (1.0 + speed))


def upwind(speed, weight, low, high, low_slope, high_slope):
    forward = speed > 0.0
    value = jnp.where(forward, low, high)
    slope = jnp.where(forward, low_slope, high_slope)
    return speed * (value + weight * slope)


def in_batches(lo, hi, width, work):
    steps = (hi - lo) // width
    if steps == 1:
        work([lo + part for part in range(width)])
    elif steps > 1:
        pl.loop(0, steps)(lambda step: work([lo + width * step + part for part in range(width)]))
    if lo + steps * width < hi:
        work(list(range(lo + steps * width, hi)))


def running_sum(values, stride):
    rows = values.shape[0]
    index = lax.broadcasted_iota(jnp.int32, values.shape, 0)
    shift = stride
    while shift < rows:
        moved = pltpu.roll(values, shift, 0)
        values = values + jnp.where(index >= shift, moved, 0.0)
        shift *= 2
    return values


def kernel(
    tr,
    fl,
    ts,
    wt,
    acc,
    heat,
    mom,
    q,
    flow,
    wet_raw,
    wet,
    halo,
    edge_out,
    edge,
    pack,
    pack_in,
    line,
    side,
    cz,
    hz,
    cx,
    hx,
    cy,
    hy,
    growth,
    absorbed,
    fz,
    sz,
    nbr,
    transit,
    load_sem,
    pack_send,
    pack_recv,
    send_sem,
    recv_sem,
    relay_send,
    relay_recv,
    go,
):
    tracers = tr.shape[0]
    fields = tracers + 2
    rows = q.shape[1] - 2 * PAD
    levels = rows // 2
    temp, salt = tracers, tracers + 1
    pieces = piece_list(tracers)
    whole = slice(PAD, PAD + rows)

    grp, gx, gy = lax.axis_index("grp"), lax.axis_index("gx"), lax.axis_index("gy")
    n_grp, n_gx, n_gy = lax.axis_size("grp"), lax.axis_size("gx"), lax.axis_size("gy")
    lon, n_lon = grp * n_gx + gx, n_grp * n_gx

    def place(index):
        return index // n_gx, index % n_gx

    def depth(index):
        return (index % n_gx) // (n_gx // 2) * n_grp + index // n_gx

    right_lon = (lon + 1) % n_lon
    left_lon = (lon + n_lon - 1) % n_lon
    mirror_lon = n_lon - 1 - lon
    right, left = (*place(right_lon), gy), (*place(left_lon), gy)
    north, south = (grp, gx, jnp.minimum(gy + 1, n_gy - 1)), (grp, gx, jnp.maximum(gy - 1, 0))
    partner = (*place(mirror_lon), n_gy - 1)
    carrier_row = min(1, n_gy - 2)
    carrier = (*place(mirror_lon), carrier_row)
    own_top, own_carrier = (grp, gx, n_gy - 1), (grp, gx, carrier_row)
    is_top, has_south = gy == n_gy - 1, gy > 0
    has_north = gy < n_gy - 1
    here, over_right, over_left = depth(lon), depth(right_lon), depth(left_lon)
    early_right, early_left = here < over_right, here < over_left
    late_right, late_left = here > over_right, here > over_left
    early_fold = here < depth(mirror_lon)
    answers = is_top & early_fold
    opens = is_top & jnp.logical_not(early_fold)
    relays = gy == carrier_row
    waits_east_west = early_right | early_left
    mesh_id = pl.DeviceIdType.MESH

    barrier = pltpu.get_barrier_semaphore()

    def greet(condition, other):
        @pl.when(condition)
        def _():
            pl.semaphore_signal(barrier, inc=1, device_id=other, device_id_type=mesh_id)

    greet(answers, partner)
    greet(is_top, own_carrier)
    greet(relays & early_fold, partner)
    greet(relays & jnp.logical_not(early_fold), own_top)
    greet(has_north, north)
    greet(has_south, south)
    greet(jnp.logical_not(late_right), right)
    greet(jnp.logical_not(late_left), left)

    def one(condition):
        return jnp.where(condition, 1, 0)

    expected = one(has_north) + one(has_south) + one(opens) * 3 + one(relays)
    expected += one(jnp.logical_not(early_right)) + one(jnp.logical_not(early_left))

    loads = [
        pltpu.make_async_copy(wt, wet_raw, load_sem.at[0]),
        pltpu.make_async_copy(fl, flow.at[:, whole], load_sem.at[1]),
        pltpu.make_async_copy(ts, q.at[tracers:fields, whole], load_sem.at[2]),
        pltpu.make_async_copy(tr, q.at[0:tracers, whole], load_sem.at[3]),
    ]
    for load in loads:
        load.start()

    def piece(number, way, slot, device):
        kind, lo, hi, _ = pieces[number]
        if kind == EDGE:
            source, target = edge_out.at[way], edge.at[slot]
        elif kind == TEMP_SALT:
            source, target = ts, halo.at[slot, lo:hi]
        else:
            source, target = tr.at[lo:hi], halo.at[slot, lo:hi]
        return pltpu.make_async_remote_copy(
            source,
            target,
            send_sem.at[way, number],
            recv_sem.at[slot, number],
            device,
            mesh_id,
        )

    relayed = [number for number, entry in enumerate(pieces) if entry[3]]
    berth, total = {}, 0
    for number in relayed:
        berth[number] = total
        total += pieces[number][2] - pieces[number][1]

    def to_carrier(number):
        _, lo, hi, _ = pieces[number]
        start = berth[number]
        return pltpu.make_async_remote_copy(
            tr.at[lo:hi],
            transit.at[start : start + hi - lo],
            send_sem.at[0, number],
            relay_recv.at[number],
            carrier,
            mesh_id,
        )

    def from_carrier(number):
        _, lo, hi, _ = pieces[number]
        start = berth[number]
        return pltpu.make_async_remote_copy(
            transit.at[start : start + hi - lo],
            halo.at[1, lo:hi],
            relay_send.at[number],
            recv_sem.at[1, number],
            own_top,
            mesh_id,
        )

    def send(number):
        @pl.when(has_north)
        def _():
            piece(number, 0, 0, north).start()

        @pl.when(has_south)
        def _():
            piece(number, 1, 1, south).start()

    def open_fold(number):
        @pl.when(opens)
        def _():
            if number in berth:
                to_carrier(number).start()
            else:
                piece(number, 0, 1, partner).start()

    pl.semaphore_wait(barrier, expected)

    def permit(condition, slot, other):
        @pl.when(condition)
        def _():
            pl.semaphore_signal(go.at[slot], inc=1, device_id=other, device_id_type=mesh_id)

    permit(opens, 2, partner)
    permit(late_right, 1, right)
    permit(late_left, 0, left)
    for number in (1, relayed[0]):
        open_fold(number)

    lane = lax.broadcasted_iota(jnp.int32, (rows, LANES), 1)
    quad = lane // 4
    spot = lane % 4
    first, last = lane == 0, lane == LANES - 1

    def row_of(ref, r):
        return ref[pl.ds(r, levels, stride=2), :]

    for load in loads:
        load.wait()
    wet[whole] = wet_raw[...].astype(jnp.float32)
    for way, r in ((0, 1), (1, 0)):
        for slot in range(2):
            edge_out[way, slot] = flow[slot, pl.ds(PAD + r, levels, stride=2), :]
        edge_out[way, 2] = wet[pl.ds(PAD + r, levels, stride=2), :]

    def take(step, packed):
        for part in range(3):
            f = 3 * step + part
            turned = pltpu.roll(q[f, whole], 4 * f + 2, 1)
            packed = jnp.where(quad == f, turned, packed)
        return packed

    packed = jnp.zeros((rows, LANES), jnp.float32)
    packed = lax.fori_loop(0, fields // 3, take, packed)
    for slot in range(3):
        f = fields + slot
        packed = jnp.where(quad == f, pltpu.roll(flow[slot, whole], 4 * f + 2, 1), packed)
    f = fields + 3
    packed = jnp.where(quad == f, pltpu.roll(wet[whole], 4 * f + 2, 1), packed)
    pack[...] = packed

    zeros = jnp.zeros((PAD, LANES), jnp.float32)
    below = slice(PAD + rows, PAD + rows + PAD)
    scraps = [ref.at[part] for ref in (fz, sz) for part in range(3)]
    for pads in (wet, flow.at[0], *scraps):
        pads[0:PAD] = zeros
        pads[below] = zeros

    @pl.loop(0, fields)
    def _(f):
        q[f, 0:PAD] = zeros
        q[f, below] = zeros

    to_right = pltpu.make_async_remote_copy(
        pack, pack_in.at[0], pack_send.at[0], pack_recv.at[0], right, mesh_id
    )
    to_left = pltpu.make_async_remote_copy(
        pack, pack_in.at[1], pack_send.at[1], pack_recv.at[1], left, mesh_id
    )

    @pl.when(jnp.logical_not(early_right))
    def _():
        to_right.start()

    @pl.when(jnp.logical_not(early_left))
    def _():
        to_left.start()

    for number in range(len(pieces)):
        if number not in (1, relayed[0]):
            open_fold(number)
    for number in range(len(pieces)):
        send(number)

    @pl.when(jnp.logical_not(has_south))
    def _():
        edge[0] = jnp.zeros((3, levels, LANES), jnp.float32)

        @pl.loop(0, fields)
        def _(f):
            halo[0, f] = jnp.zeros((rows, LANES), jnp.float32)

    mirror = LANES - 1 - lax.broadcasted_iota(jnp.int32, (levels, LANES), 1)

    def flip(values):
        return jnp.take_along_axis(values, mirror, axis=1)

    def await_piece(number):
        kind, lo, hi, _ = pieces[number]

        @pl.when(has_south)
        def _():
            piece(number, 0, 0, south).wait_recv()

        piece(number, 1, 1, south).wait_recv()

        @pl.when(is_top)
        def _():
            if kind == EDGE:
                edge[1, 0] = -flip(edge[1, 0])
                edge[1, 1] = -flip(edge[1, 1])
                edge[1, 2] = flip(edge[1, 2])
            else:

                def turn(batch):
                    rims = [(halo.at[1, f], r) for f in batch for r in range(2)]
                    turned = [flip(row_of(there, r)) for there, r in rims]
                    for (there, r), value in zip(rims, turned):
                        there[pl.ds(1 - r, levels, stride=2), :] = value

                in_batches(lo, hi, 2, turn)

    wet_here = wet[whole]

    speed = 0.5 * (flow[0, whole] + flow[0, PAD + 2 : PAD + 2 + rows])
    speed = speed * wet_here * wet[PAD + 2 : PAD + 2 + rows]
    cz[...] = speed
    hz[...] = face_terms(speed)

    attenuation = wet_here * (light_water + light_chloro * q[1, whole])
    light_top = jnp.exp(-(running_sum(attenuation, 2) - attenuation))
    absorbed[...] = light_top * (1.0 - jnp.exp(-attenuation))
    growth[...] = (
        highest_division_speed
        * jnp.exp(thermal_multiplier * q[temp, whole])
        * light_top
        / (photic_halfway_level + light_top)
    )

    def beyond(ref, f):
        return pltpu.roll(ref[...], LANES - 2 - 4 * f, 1)

    def east(values, outer):
        return pltpu.roll(jnp.where(first, outer, values), LANES - 1, 1)

    def west(values, outer):
        return pltpu.roll(jnp.where(last, outer, values), 1, 1)

    def along_levels(batch):
        values = [q[f, whole] for f in batch]
        deeper = [q[f, PAD + 2 : PAD + 2 + rows] for f in batch]
        slopes = [
            minmod(d - v, v - q[f, PAD - 2 : PAD - 2 + rows])
            for d, v, f in zip(deeper, values, batch)
        ]
        for part, slope in enumerate(slopes):
            sz[part, whole] = slope
        fluxes = [
            upwind(cz[...], hz[...], v, d, slope, sz[part, PAD + 2 : PAD + 2 + rows])
            for part, (v, d, slope) in enumerate(zip(values, deeper, slopes))
        ]
        for part, flux in enumerate(fluxes):
            fz[part, whole] = flux
        for part, (f, v, flux) in enumerate(zip(batch, values, fluxes)):
            acc[f] = v - (flux - fz[part, PAD - 2 : PAD - 2 + rows])

    in_batches(0, fields, 3, along_levels)

    def reply_east_west():
        @pl.when(early_right)
        def _():
            pl.semaphore_wait(go.at[0], 1)
            to_right.start()

        @pl.when(early_left)
        def _():
            pl.semaphore_wait(go.at[1], 1)
            to_left.start()

    def forward(part, parts):
        @pl.when(relays)
        def _():
            for number in relayed[part * len(relayed) // parts : (part + 1) * len(relayed) // parts]:
                to_carrier(number).wait_recv()
                from_carrier(number).start()

    def along_longitude(carrying=False):
        to_right.wait_recv()
        to_left.wait_recv()
        own = pack[...]
        lines = jnp.where(spot < 2, pack_in[0], pack_in[1])
        line[...] = lines
        wet_here = wet[whole]
        eastward = flow[2, whole]
        outer_wet = beyond(line, fields + 3)
        outer_flow = beyond(line, fields + 2)
        wet_east, wet_west = east(wet_here, outer_wet), west(wet_here, outer_wet)
        speed = 0.5 * (eastward + east(eastward, outer_flow)) * wet_here * wet_east
        cx[...] = speed
        hx[...] = face_terms(speed)
        entry = 0.5 * (west(eastward, outer_flow) + eastward) * wet_west * wet_here
        entry = jnp.broadcast_to(entry[:, 0:1], (rows, LANES))

        low_line = jnp.where(spot < 2, lines, own)
        low_next = pltpu.roll(low_line, LANES - 1, 1)
        gap = low_next - low_line
        low_slope = minmod(gap, pltpu.roll(gap, 1, 1))
        entry_flux = upwind(
            entry,
            face_terms(entry),
            low_line,
            low_next,
            low_slope,
            pltpu.roll(low_slope, LANES - 1, 1),
        )
        high_line = jnp.where(spot < 2, own, lines)
        gap = pltpu.roll(high_line, LANES - 1, 1) - high_line
        high_slope = minmod(gap, pltpu.roll(gap, 1, 1))
        side[...] = jnp.where(spot == 1, entry_flux, high_slope)

        def some_fields(step):
            batch = [3 * step + part for part in range(3)]
            before = [acc[f] for f in batch]
            values = [q[f, whole] for f in batch]
            outers = [beyond(line, f) for f in batch]
            sides = [beyond(side, f) for f in batch]
            nexts = [east(v, o) for v, o in zip(values, outers)]
            slopes = [
                minmod(n - v, v - west(v, o)) for n, v, o in zip(nexts, values, outers)
            ]
            fluxes = [
                upwind(cx[...], hx[...], v, n, slope, east(slope, outer_side))
                for v, n, slope, outer_side in zip(values, nexts, slopes, sides)
            ]
            for f, old, flux, outer_side in zip(batch, before, fluxes, sides):
                acc[f] = old - (flux - west(flux, outer_side))

        parts, batches = 4 if carrying else 1, fields // 3
        for part in range(parts):
            pl.loop(part * batches // parts, (part + 1) * batches // parts)(some_fields)
            if carrying:
                forward(part, parts)

    @pl.when(jnp.logical_not(waits_east_west))
    def _():
        along_longitude()

    @pl.when(waits_east_west & is_top)
    def _():
        reply_east_west()

    @pl.when(answers)
    def _():
        pl.semaphore_wait(go.at[2], 1)
        for number in range(len(pieces)):
            if number in berth:
                to_carrier(number).start()
            else:
                piece(number, 0, 1, partner).start()

    @pl.when(waits_east_west & is_top)
    def _():
        along_longitude()

    await_piece(0)
    own_rows = [wet[pl.ds(PAD + r, levels, stride=2), :] for r in range(2)]
    wets = [edge[0, 2]] + own_rows + [edge[1, 2]]
    flows = [edge[0, 1]]
    flows += [flow[1, pl.ds(PAD + r, levels, stride=2), :] for r in range(2)]
    flows += [edge[1, 1]]
    for face in range(3):
        speed = 0.5 * (flows[face] + flows[face + 1]) * wets[face] * wets[face + 1]
        cy[face] = speed
        hy[face] = face_terms(speed)

    def across(f):
        results = []
        for block in range(levels // 8):
            span = slice(8 * block, 8 * block + 8)

            def load(ref, start, r):
                return ref[pl.ds(start + 16 * block + r, 8, stride=2), :]

            here = q.at[f]
            values = [load(halo.at[0, f], 0, 0), load(halo.at[0, f], 0, 1)]
            values += [load(here, PAD, 0), load(here, PAD, 1)]
            values += [load(halo.at[1, f], 0, 0), load(halo.at[1, f], 0, 1)]
            gaps = [values[i + 1] - values[i] for i in range(5)]
            slopes = [minmod(gaps[i + 1], gaps[i]) for i in range(4)]
            fluxes = [
                upwind(
                    cy[i, span],
                    hy[i, span],
                    values[i + 1],
                    values[i + 2],
                    slopes[i],
                    slopes[i + 1],
                )
                for i in range(3)
            ]
            for r in range(2):
                target = (f, pl.ds(16 * block + r, 8, stride=2), slice(None))
                results.append((target, acc[target] - (fluxes[r + 1] - fluxes[r])))
        return results

    def across_all(batch):
        for target, value in [entry for f in batch for entry in across(f)]:
            acc[target] = value

    def rows_of_piece(number):
        await_piece(number)
        _, lo, hi, _ = pieces[number]

        in_batches(lo, hi, 2, across_all)

    def finish():
        wet_here = wet[whole]
        outer_wet = beyond(line, fields + 3)
        wet_east, wet_west = east(wet_here, outer_wet), west(wet_here, outer_wet)
        heat[0] = acc[temp] + heat_gain * absorbed[...]
        heat[1] = acc[salt]

        def weigh(wetness, heat, salinity):
            return wetness * (rho_temp * heat + rho_salt * salinity)

        def pressure_of(density, stride):
            return running_sum(density, stride) - 0.5 * density

        press = pressure_of(weigh(wet_here, q[temp, whole], q[salt, whole]), 2)
        outer_press = pressure_of(weigh(outer_wet, beyond(line, temp), beyond(line, salt)), 2)
        press_south = pressure_of(
            weigh(edge[0, 2], row_of(halo.at[0, temp], 1), row_of(halo.at[0, salt], 1)), 1
        )
        press_north = pressure_of(
            weigh(edge[1, 2], row_of(halo.at[1, temp], 0), row_of(halo.at[1, salt], 0)), 1
        )
        nbr[2] = press

        def spread(slot, own_ref, start, lower, upper):
            nbr[0, pl.ds(0, levels, stride=2), :] = lower
            nbr[0, pl.ds(1, levels, stride=2), :] = own_ref[pl.ds(start, levels, stride=2), :]
            nbr[1, pl.ds(0, levels, stride=2), :] = own_ref[pl.ds(start + 1, levels, stride=2), :]
            nbr[1, pl.ds(1, levels, stride=2), :] = upper
            return nbr[1], nbr[0]

        wet_north, wet_south = spread(0, wet, PAD, edge[0, 2], edge[1, 2])
        near_wet = (wet_east, wet_west, wet_north, wet_south)
        press_n, press_s = spread(1, nbr.at[2], 0, press_south, press_north)
        near = (east(press, outer_press), west(press, outer_press), press_n, press_s)
        near = [w * p + (1.0 - w) * press for w, p in zip(near_wet, near)]
        grad_x = 0.5 * (near[0] - near[1])
        grad_y = 0.5 * (near[2] - near[3])

        def laplace(slot):
            values = flow[slot, whole]
            outer = beyond(line, fields + slot)
            up, down = spread(slot, flow.at[slot], PAD, edge[0, slot], edge[1, slot])
            near_values = (east(values, outer), west(values, outer), up, down)
            total = near_wet[0] * near_values[0]
            for w, value in zip(near_wet[1:], near_values[1:]):
                total = total + w * value
            return total - 4.0 * values

        zonal, merid = flow[0, whole], flow[1, whole]
        mom[0] = wet_here * (
            zonal + time_step * (coriolis * merid - grad_x) + viscosity * laplace(0)
        )
        mom[1] = wet_here * (
            merid + time_step * (-coriolis * zonal - grad_y) + viscosity * laplace(1)
        )
        @pl.loop(0, rows // 32)
        def _(block):
            span = pl.ds(pl.multiple_of(32 * block, 8), 32)
            wet_span = pl.ds(pl.multiple_of(32 * block + PAD, 8), 32)
            nutrient, phyto, zoo, detritus = [acc[i, span] for i in range(4)]
            speed = growth[span]
            step = bio_step * wet[wet_span]
            for _ in range(SUBSTEPS):
                uptake = speed * nutrient / (half_nutrient + jnp.abs(nutrient)) * phyto
                square = phyto * phyto
                grazing = zoo * square / (half_prey + square)
                nutrient_next = nutrient + step * (remin_rate * detritus - uptake)
                phyto_next = phyto + step * (uptake - grazing - phyto_loss * phyto)
                zoo_next = zoo + step * (graze_yield * grazing - zoo_loss * zoo)
                detritus = detritus + step * (
                    (1.0 - graze_yield) * grazing
                    + phyto_loss * phyto
                    + zoo_loss * zoo
                    - remin_rate * detritus
                )
                nutrient, phyto, zoo = nutrient_next, phyto_next, zoo_next
            for i, value in enumerate((nutrient, phyto, zoo, detritus)):
                acc[i, span] = value


    for number in (1, 2):
        rows_of_piece(number)

    @pl.when(jnp.logical_not(waits_east_west) | is_top)
    def _():
        finish()

    for number in range(3, len(pieces)):
        rows_of_piece(number)

    @pl.when(waits_east_west & has_north)
    def _():
        reply_east_west()
        along_longitude(carrying=True)
        finish()

    @pl.when(jnp.logical_not(waits_east_west))
    def _():
        forward(0, 1)

    @pl.when(relays)
    def _():
        for number in relayed:
            from_carrier(number).wait_send()

    to_right.wait_send()
    to_left.wait_send()
    for number in range(len(pieces)):
        piece(number, 0, 0, north).wait_send()

        @pl.when(has_south)
        def _():
            piece(number, 1, 1, south).wait_send()


def write_out(acc, heat, mom, otr, ots, ofl, sem):
    outs = [
        pltpu.make_async_copy(acc.at[0 : otr.shape[0]], otr, sem.at[0]),
        pltpu.make_async_copy(heat, ots, sem.at[1]),
        pltpu.make_async_copy(mom, ofl, sem.at[2]),
    ]
    for out in outs:
        out.start()
    for out in outs:
        out.wait()


def body(tracers, flow, temp_salt, wet):
    count, levels, height, breadth = tracers.shape
    rows = levels * height
    fields = count + 2
    entries = piece_list(count)
    pieces = len(entries)
    moored = sum(hi - lo for _, lo, hi, relay in entries if relay)
    f32 = jnp.float32
    field = pltpu.VMEM((rows, breadth), f32)
    padded = pltpu.VMEM((rows + 2 * PAD, breadth), f32)
    dma = pltpu.SemaphoreType.DMA
    anywhere = pl.BlockSpec(memory_space=pl.ANY)
    local = pl.BlockSpec(memory_space=pltpu.VMEM)
    pair = (2, rows, breadth)
    results = pl.pallas_call(
        kernel,
        out_shape=(
            pltpu.VMEM((fields, rows, breadth), f32),
            pltpu.VMEM(pair, f32),
            pltpu.VMEM(pair, f32),
        ),
        in_specs=[anywhere] * 4,
        out_specs=(local,) * 3,
        scratch_shapes=[
            pltpu.VMEM((fields, rows + 2 * PAD, breadth), f32),
            pltpu.VMEM((3, rows + 2 * PAD, breadth), f32),
            pltpu.VMEM((rows, breadth), jnp.int32),
            padded,
            pltpu.VMEM((2, fields, rows, breadth), f32),
            pltpu.VMEM((2, 3, levels, breadth), f32),
            pltpu.VMEM((2, 3, levels, breadth), f32),
            field,
            pltpu.VMEM(pair, f32),
            field,
            field,
            field,
            field,
            field,
            field,
            pltpu.VMEM((3, levels, breadth), f32),
            pltpu.VMEM((3, levels, breadth), f32),
            field,
            field,
            pltpu.VMEM((3, rows + 2 * PAD, breadth), f32),
            pltpu.VMEM((3, rows + 2 * PAD, breadth), f32),
            pltpu.VMEM((3, rows, breadth), f32),
            pltpu.VMEM((max(1, moored), rows, breadth), f32),
            dma((4,)),
            dma((2,)),
            dma((2,)),
            dma((2, pieces)),
            dma((2, pieces)),
            dma((pieces,)),
            dma((pieces,)),
            pltpu.SemaphoreType.REGULAR((3,)),
        ],
        compiler_params=pltpu.CompilerParams(collective_id=0, has_side_effects=True),
        name="step",
    )(
        tracers.reshape(count, rows, breadth),
        flow.reshape(3, rows, breadth),
        temp_salt.reshape(2, rows, breadth),
        wet.reshape(rows, breadth),
    )
    outs = pl.pallas_call(
        write_out,
        out_shape=(
            jax.ShapeDtypeStruct((count, rows, breadth), f32),
            jax.ShapeDtypeStruct(pair, f32),
            jax.ShapeDtypeStruct(pair, f32),
        ),
        in_specs=[local] * 3,
        out_specs=(anywhere,) * 3,
        scratch_shapes=[dma((3,))],
        name="write_out",
    )(*(pltpu.with_memory_space_constraint(value, pltpu.VMEM) for value in results))
    return tuple(out.reshape(-1, levels, height, breadth) for out in outs)


def solution(mesh):
    four = P(None, None, "gy", ("grp", "gx"))
    return jax.shard_map(
        body,
        mesh=mesh,
        in_specs=(four, four, four, P(None, "gy", ("grp", "gx"))),
        out_specs=(four, four, four),
        check_vma=False,
    )
```

```python
import functools

import jax
import jax.numpy as jnp
from jax import lax
from jax.experimental import pallas as pl
from jax.experimental.pallas import tpu as pltpu
from jax.sharding import PartitionSpec as P

SUBSTEPS = 4
light_water = 0.04
light_chloro = 0.06
rho_temp = -0.2
rho_salt = 0.8
time_step = 0.02
coriolis = 0.4
viscosity = 0.1
heat_gain = 4.0
photic_halfway_level = 0.2
highest_division_speed = 1.5
half_nutrient = 0.5
half_prey = 0.3
phyto_loss = 0.05
zoo_loss = 0.1
graze_yield = 0.3
remin_rate = 0.15
bio_step = 0.25
thermal_multiplier = 0.063

LANES = 128
PAD = 8


EDGE, TEMP_SALT = "edge", "temp_salt"


def piece_list(tracers):
    pieces = [(EDGE, 0, 0, 0), (TEMP_SALT, tracers, tracers + 2, 0), ("tracers", 0, 4, 0)]
    plan = ((3, 1), (3, 2), (2, 0), (2, 1), (2, 2), (2, 1), (tracers, 2))
    start = 4
    for size, route in plan:
        stop = min(tracers, start + size)
        if stop > start:
            pieces.append(("tracers", start, stop, route))
        start = stop
    return pieces


def minmod(former, latter):
    return jnp.maximum(
        jnp.minimum(former, latter), jnp.minimum(jnp.maximum(former, latter), 0.0)
    )


def face_terms(speed):
    return jnp.where(speed > 0.0, 0.5 * (1.0 - speed), -0.5 * (1.0 + speed))


def upwind(speed, weight, low, high, low_slope, high_slope):
    forward = speed > 0.0
    value = jnp.where(forward, low, high)
    slope = jnp.where(forward, low_slope, high_slope)
    return speed * (value + weight * slope)


def in_batches(lo, hi, width, work):
    steps = (hi - lo) // width
    if steps == 1:
        work([lo + part for part in range(width)])
    elif steps > 1:
        pl.loop(0, steps)(lambda step: work([lo + width * step + part for part in range(width)]))
    if lo + steps * width < hi:
        work(list(range(lo + steps * width, hi)))


def running_sum(values, stride):
    rows = values.shape[0]
    index = lax.broadcasted_iota(jnp.int32, values.shape, 0)
    shift = stride
    while shift < rows:
        moved = pltpu.roll(values, shift, 0)
        values = values + jnp.where(index >= shift, moved, 0.0)
        shift *= 2
    return values


def kernel(
    tr,
    fl,
    ts,
    wt,
    acc,
    heat,
    mom,
    q,
    flow,
    wet_raw,
    wet,
    halo,
    edge_out,
    edge,
    pack,
    pack_in,
    line,
    side,
    cz,
    hz,
    cx,
    hx,
    cy,
    hy,
    growth,
    absorbed,
    fz,
    sz,
    nbr,
    transit,
    load_sem,
    pack_send,
    pack_recv,
    send_sem,
    recv_sem,
    relay_send,
    relay_recv,
    go,
):
    tracers = tr.shape[0]
    fields = tracers + 2
    rows = q.shape[1] - 2 * PAD
    levels = rows // 2
    temp, salt = tracers, tracers + 1
    pieces = piece_list(tracers)
    whole = slice(PAD, PAD + rows)

    grp, gx, gy = lax.axis_index("grp"), lax.axis_index("gx"), lax.axis_index("gy")
    n_grp, n_gx, n_gy = lax.axis_size("grp"), lax.axis_size("gx"), lax.axis_size("gy")
    lon, n_lon = grp * n_gx + gx, n_grp * n_gx

    def place(index):
        return index // n_gx, index % n_gx

    def depth(index):
        return (index % n_gx) // (n_gx // 2) * n_grp + index // n_gx

    right_lon = (lon + 1) % n_lon
    left_lon = (lon + n_lon - 1) % n_lon
    mirror_lon = n_lon - 1 - lon
    right, left = (*place(right_lon), gy), (*place(left_lon), gy)
    north, south = (grp, gx, jnp.minimum(gy + 1, n_gy - 1)), (grp, gx, jnp.maximum(gy - 1, 0))
    partner = (*place(mirror_lon), n_gy - 1)
    carrier_rows = (min(1, n_gy - 2), max(0, n_gy - 4))
    carriers = [(*place(mirror_lon), r) for r in carrier_rows]
    own_carriers = [(grp, gx, r) for r in carrier_rows]
    own_top = (grp, gx, n_gy - 1)
    is_top, has_south = gy == n_gy - 1, gy > 0
    has_north = gy < n_gy - 1
    here, over_right, over_left = depth(lon), depth(right_lon), depth(left_lon)
    early_right, early_left = here < over_right, here < over_left
    late_right, late_left = here > over_right, here > over_left
    early_fold = here < depth(mirror_lon)
    answers = is_top & early_fold
    opens = is_top & jnp.logical_not(early_fold)
    carries = [gy == r for r in carrier_rows]
    relays = carries[0] | carries[1]
    waits_east_west = early_right | early_left
    mesh_id = pl.DeviceIdType.MESH

    barrier = pltpu.get_barrier_semaphore()

    def greet(condition, other):
        @pl.when(condition)
        def _():
            pl.semaphore_signal(barrier, inc=1, device_id=other, device_id_type=mesh_id)

    greet(answers, partner)
    for other in own_carriers:
        greet(is_top, other)
    greet(relays & early_fold, partner)
    greet(relays & jnp.logical_not(early_fold), own_top)
    greet(has_north, north)
    greet(has_south, south)
    greet(jnp.logical_not(late_right), right)
    greet(jnp.logical_not(late_left), left)

    def one(condition):
        return jnp.where(condition, 1, 0)

    expected = one(has_north) + one(has_south) + one(opens) * 5 + one(relays)
    expected += one(jnp.logical_not(early_right)) + one(jnp.logical_not(early_left))

    loads = [
        pltpu.make_async_copy(wt, wet_raw, load_sem.at[0]),
        pltpu.make_async_copy(fl, flow.at[:, whole], load_sem.at[1]),
        pltpu.make_async_copy(ts, q.at[tracers:fields, whole], load_sem.at[2]),
        pltpu.make_async_copy(tr, q.at[0:tracers, whole], load_sem.at[3]),
    ]
    for load in loads:
        load.start()

    def piece(number, way, slot, device):
        kind, lo, hi, _ = pieces[number]
        if kind == EDGE:
            source, target = edge_out.at[way], edge.at[slot]
        elif kind == TEMP_SALT:
            source, target = ts, halo.at[slot, lo:hi]
        else:
            source, target = tr.at[lo:hi], halo.at[slot, lo:hi]
        return pltpu.make_async_remote_copy(
            source,
            target,
            send_sem.at[way, number],
            recv_sem.at[slot, number],
            device,
            mesh_id,
        )

    relayed = [number for number, entry in enumerate(pieces) if entry[3]]
    berth, total = {}, 0
    for number in relayed:
        berth[number] = total
        total += pieces[number][2] - pieces[number][1]

    def to_carrier(number):
        _, lo, hi, _ = pieces[number]
        start = berth[number]
        return pltpu.make_async_remote_copy(
            tr.at[lo:hi],
            transit.at[start : start + hi - lo],
            send_sem.at[0, number],
            relay_recv.at[number],
            carriers[pieces[number][3] - 1],
            mesh_id,
        )

    def from_carrier(number):
        _, lo, hi, _ = pieces[number]
        start = berth[number]
        return pltpu.make_async_remote_copy(
            transit.at[start : start + hi - lo],
            halo.at[1, lo:hi],
            relay_send.at[number],
            recv_sem.at[1, number],
            own_top,
            mesh_id,
        )

    def send(number):
        @pl.when(has_north)
        def _():
            piece(number, 0, 0, north).start()

        @pl.when(has_south)
        def _():
            piece(number, 1, 1, south).start()

    def open_fold(number):
        @pl.when(opens)
        def _():
            if number in berth:
                to_carrier(number).start()
            else:
                piece(number, 0, 1, partner).start()

    pl.semaphore_wait(barrier, expected)

    def permit(condition, slot, other):
        @pl.when(condition)
        def _():
            pl.semaphore_signal(go.at[slot], inc=1, device_id=other, device_id_type=mesh_id)

    permit(opens, 2, partner)
    permit(late_right, 1, right)
    permit(late_left, 0, left)
    opening = (1, *relayed[:2])
    for number in opening:
        open_fold(number)

    lane = lax.broadcasted_iota(jnp.int32, (rows, LANES), 1)
    quad = lane // 4
    spot = lane % 4
    first, last = lane == 0, lane == LANES - 1

    def row_of(ref, r):
        return ref[pl.ds(r, levels, stride=2), :]

    for load in loads:
        load.wait()
    wet[whole] = wet_raw[...].astype(jnp.float32)
    for way, r in ((0, 1), (1, 0)):
        for slot in range(2):
            edge_out[way, slot] = flow[slot, pl.ds(PAD + r, levels, stride=2), :]
        edge_out[way, 2] = wet[pl.ds(PAD + r, levels, stride=2), :]

    def take(step, packed):
        for part in range(3):
            f = 3 * step + part
            turned = pltpu.roll(q[f, whole], 4 * f + 2, 1)
            packed = jnp.where(quad == f, turned, packed)
        return packed

    packed = jnp.zeros((rows, LANES), jnp.float32)
    packed = lax.fori_loop(0, fields // 3, take, packed)
    for slot in range(3):
        f = fields + slot
        packed = jnp.where(quad == f, pltpu.roll(flow[slot, whole], 4 * f + 2, 1), packed)
    f = fields + 3
    packed = jnp.where(quad == f, pltpu.roll(wet[whole], 4 * f + 2, 1), packed)
    pack[...] = packed

    zeros = jnp.zeros((PAD, LANES), jnp.float32)
    below = slice(PAD + rows, PAD + rows + PAD)
    scraps = [ref.at[part] for ref in (fz, sz) for part in range(3)]
    for pads in (wet, flow.at[0], *scraps):
        pads[0:PAD] = zeros
        pads[below] = zeros

    @pl.loop(0, fields)
    def _(f):
        q[f, 0:PAD] = zeros
        q[f, below] = zeros

    to_right = pltpu.make_async_remote_copy(
        pack, pack_in.at[0], pack_send.at[0], pack_recv.at[0], right, mesh_id
    )
    to_left = pltpu.make_async_remote_copy(
        pack, pack_in.at[1], pack_send.at[1], pack_recv.at[1], left, mesh_id
    )

    @pl.when(jnp.logical_not(early_right))
    def _():
        to_right.start()

    @pl.when(jnp.logical_not(early_left))
    def _():
        to_left.start()

    for number in range(len(pieces)):
        if number not in opening:
            open_fold(number)
    for number in range(len(pieces)):
        send(number)

    @pl.when(jnp.logical_not(has_south))
    def _():
        edge[0] = jnp.zeros((3, levels, LANES), jnp.float32)

        @pl.loop(0, fields)
        def _(f):
            halo[0, f] = jnp.zeros((rows, LANES), jnp.float32)

    mirror = LANES - 1 - lax.broadcasted_iota(jnp.int32, (levels, LANES), 1)

    def flip(values):
        return jnp.take_along_axis(values, mirror, axis=1)

    def await_piece(number):
        kind, lo, hi, _ = pieces[number]

        @pl.when(has_south)
        def _():
            piece(number, 0, 0, south).wait_recv()

        piece(number, 1, 1, south).wait_recv()

        @pl.when(is_top)
        def _():
            if kind == EDGE:
                edge[1, 0] = -flip(edge[1, 0])
                edge[1, 1] = -flip(edge[1, 1])
                edge[1, 2] = flip(edge[1, 2])
            else:

                def turn(batch):
                    rims = [(halo.at[1, f], r) for f in batch for r in range(2)]
                    turned = [flip(row_of(there, r)) for there, r in rims]
                    for (there, r), value in zip(rims, turned):
                        there[pl.ds(1 - r, levels, stride=2), :] = value

                in_batches(lo, hi, 2, turn)

    wet_here = wet[whole]

    speed = 0.5 * (flow[0, whole] + flow[0, PAD + 2 : PAD + 2 + rows])
    speed = speed * wet_here * wet[PAD + 2 : PAD + 2 + rows]
    cz[...] = speed
    hz[...] = face_terms(speed)

    attenuation = wet_here * (light_water + light_chloro * q[1, whole])
    light_top = jnp.exp(-(running_sum(attenuation, 2) - attenuation))
    absorbed[...] = light_top * (1.0 - jnp.exp(-attenuation))
    growth[...] = (
        highest_division_speed
        * jnp.exp(thermal_multiplier * q[temp, whole])
        * light_top
        / (photic_halfway_level + light_top)
    )

    def beyond(ref, f):
        return pltpu.roll(ref[...], LANES - 2 - 4 * f, 1)

    def east(values, outer):
        return pltpu.roll(jnp.where(first, outer, values), LANES - 1, 1)

    def west(values, outer):
        return pltpu.roll(jnp.where(last, outer, values), 1, 1)

    def along_levels(batch):
        values = [q[f, whole] for f in batch]
        deeper = [q[f, PAD + 2 : PAD + 2 + rows] for f in batch]
        slopes = [
            minmod(d - v, v - q[f, PAD - 2 : PAD - 2 + rows])
            for d, v, f in zip(deeper, values, batch)
        ]
        for part, slope in enumerate(slopes):
            sz[part, whole] = slope
        fluxes = [
            upwind(cz[...], hz[...], v, d, slope, sz[part, PAD + 2 : PAD + 2 + rows])
            for part, (v, d, slope) in enumerate(zip(values, deeper, slopes))
        ]
        for part, flux in enumerate(fluxes):
            fz[part, whole] = flux
        for part, (f, v, flux) in enumerate(zip(batch, values, fluxes)):
            acc[f] = v - (flux - fz[part, PAD - 2 : PAD - 2 + rows])

    in_batches(0, fields, 3, along_levels)

    def reply_east_west():
        @pl.when(early_right)
        def _():
            pl.semaphore_wait(go.at[0], 1)
            to_right.start()

        @pl.when(early_left)
        def _():
            pl.semaphore_wait(go.at[1], 1)
            to_left.start()

    def forward(part, parts):
        for route, mine in enumerate(carries, 1):
            routed = [number for number in relayed if pieces[number][3] == route]

            @pl.when(mine)
            def _():
                for number in routed[part * len(routed) // parts : (part + 1) * len(routed) // parts]:
                    to_carrier(number).wait_recv()
                    from_carrier(number).start()

    def along_longitude(carrying=False):
        to_right.wait_recv()
        to_left.wait_recv()
        own = pack[...]
        lines = jnp.where(spot < 2, pack_in[0], pack_in[1])
        line[...] = lines
        wet_here = wet[whole]
        eastward = flow[2, whole]
        outer_wet = beyond(line, fields + 3)
        outer_flow = beyond(line, fields + 2)
        wet_east, wet_west = east(wet_here, outer_wet), west(wet_here, outer_wet)
        speed = 0.5 * (eastward + east(eastward, outer_flow)) * wet_here * wet_east
        cx[...] = speed
        hx[...] = face_terms(speed)
        entry = 0.5 * (west(eastward, outer_flow) + eastward) * wet_west * wet_here
        entry = jnp.broadcast_to(entry[:, 0:1], (rows, LANES))

        low_line = jnp.where(spot < 2, lines, own)
        low_next = pltpu.roll(low_line, LANES - 1, 1)
        gap = low_next - low_line
        low_slope = minmod(gap, pltpu.roll(gap, 1, 1))
        entry_flux = upwind(
            entry,
            face_terms(entry),
            low_line,
            low_next,
            low_slope,
            pltpu.roll(low_slope, LANES - 1, 1),
        )
        high_line = jnp.where(spot < 2, own, lines)
        gap = pltpu.roll(high_line, LANES - 1, 1) - high_line
        high_slope = minmod(gap, pltpu.roll(gap, 1, 1))
        side[...] = jnp.where(spot == 1, entry_flux, high_slope)

        def some_fields(step):
            batch = [3 * step + part for part in range(3)]
            before = [acc[f] for f in batch]
            values = [q[f, whole] for f in batch]
            outers = [beyond(line, f) for f in batch]
            sides = [beyond(side, f) for f in batch]
            nexts = [east(v, o) for v, o in zip(values, outers)]
            slopes = [
                minmod(n - v, v - west(v, o)) for n, v, o in zip(nexts, values, outers)
            ]
            fluxes = [
                upwind(cx[...], hx[...], v, n, slope, east(slope, outer_side))
                for v, n, slope, outer_side in zip(values, nexts, slopes, sides)
            ]
            for f, old, flux, outer_side in zip(batch, before, fluxes, sides):
                acc[f] = old - (flux - west(flux, outer_side))

        parts, batches = 3 if carrying else 1, fields // 3
        for part in range(parts):
            pl.loop(part * batches // parts, (part + 1) * batches // parts)(some_fields)
            if carrying:
                forward(part, parts)

    @pl.when(jnp.logical_not(waits_east_west))
    def _():
        along_longitude()

    @pl.when(waits_east_west & is_top)
    def _():
        reply_east_west()

    @pl.when(answers)
    def _():
        pl.semaphore_wait(go.at[2], 1)
        for number in range(len(pieces)):
            if number in berth:
                to_carrier(number).start()
            else:
                piece(number, 0, 1, partner).start()

    @pl.when(waits_east_west & is_top)
    def _():
        along_longitude()

    await_piece(0)
    own_rows = [wet[pl.ds(PAD + r, levels, stride=2), :] for r in range(2)]
    wets = [edge[0, 2]] + own_rows + [edge[1, 2]]
    flows = [edge[0, 1]]
    flows += [flow[1, pl.ds(PAD + r, levels, stride=2), :] for r in range(2)]
    flows += [edge[1, 1]]
    for face in range(3):
        speed = 0.5 * (flows[face] + flows[face + 1]) * wets[face] * wets[face + 1]
        cy[face] = speed
        hy[face] = face_terms(speed)

    def across(f):
        results = []
        for block in range(levels // 8):
            span = slice(8 * block, 8 * block + 8)

            def load(ref, start, r):
                return ref[pl.ds(start + 16 * block + r, 8, stride=2), :]

            here = q.at[f]
            values = [load(halo.at[0, f], 0, 0), load(halo.at[0, f], 0, 1)]
            values += [load(here, PAD, 0), load(here, PAD, 1)]
            values += [load(halo.at[1, f], 0, 0), load(halo.at[1, f], 0, 1)]
            gaps = [values[i + 1] - values[i] for i in range(5)]
            slopes = [minmod(gaps[i + 1], gaps[i]) for i in range(4)]
            fluxes = [
                upwind(
                    cy[i, span],
                    hy[i, span],
                    values[i + 1],
                    values[i + 2],
                    slopes[i],
                    slopes[i + 1],
                )
                for i in range(3)
            ]
            for r in range(2):
                target = (f, pl.ds(16 * block + r, 8, stride=2), slice(None))
                results.append((target, acc[target] - (fluxes[r + 1] - fluxes[r])))
        return results

    def across_all(batch):
        for target, value in [entry for f in batch for entry in across(f)]:
            acc[target] = value

    def rows_of_piece(number):
        await_piece(number)
        _, lo, hi, _ = pieces[number]

        in_batches(lo, hi, 2, across_all)

    def finish():
        wet_here = wet[whole]
        outer_wet = beyond(line, fields + 3)
        wet_east, wet_west = east(wet_here, outer_wet), west(wet_here, outer_wet)
        heat[0] = acc[temp] + heat_gain * absorbed[...]
        heat[1] = acc[salt]

        def weigh(wetness, heat, salinity):
            return wetness * (rho_temp * heat + rho_salt * salinity)

        def pressure_of(density, stride):
            return running_sum(density, stride) - 0.5 * density

        press = pressure_of(weigh(wet_here, q[temp, whole], q[salt, whole]), 2)
        outer_press = pressure_of(weigh(outer_wet, beyond(line, temp), beyond(line, salt)), 2)
        press_south = pressure_of(
            weigh(edge[0, 2], row_of(halo.at[0, temp], 1), row_of(halo.at[0, salt], 1)), 1
        )
        press_north = pressure_of(
            weigh(edge[1, 2], row_of(halo.at[1, temp], 0), row_of(halo.at[1, salt], 0)), 1
        )
        nbr[2] = press

        def spread(slot, own_ref, start, lower, upper):
            nbr[0, pl.ds(0, levels, stride=2), :] = lower
            nbr[0, pl.ds(1, levels, stride=2), :] = own_ref[pl.ds(start, levels, stride=2), :]
            nbr[1, pl.ds(0, levels, stride=2), :] = own_ref[pl.ds(start + 1, levels, stride=2), :]
            nbr[1, pl.ds(1, levels, stride=2), :] = upper
            return nbr[1], nbr[0]

        wet_north, wet_south = spread(0, wet, PAD, edge[0, 2], edge[1, 2])
        near_wet = (wet_east, wet_west, wet_north, wet_south)
        press_n, press_s = spread(1, nbr.at[2], 0, press_south, press_north)
        near = (east(press, outer_press), west(press, outer_press), press_n, press_s)
        near = [w * p + (1.0 - w) * press for w, p in zip(near_wet, near)]
        grad_x = 0.5 * (near[0] - near[1])
        grad_y = 0.5 * (near[2] - near[3])

        def laplace(slot):
            values = flow[slot, whole]
            outer = beyond(line, fields + slot)
            up, down = spread(slot, flow.at[slot], PAD, edge[0, slot], edge[1, slot])
            near_values = (east(values, outer), west(values, outer), up, down)
            total = near_wet[0] * near_values[0]
            for w, value in zip(near_wet[1:], near_values[1:]):
                total = total + w * value
            return total - 4.0 * values

        zonal, merid = flow[0, whole], flow[1, whole]
        mom[0] = wet_here * (
            zonal + time_step * (coriolis * merid - grad_x) + viscosity * laplace(0)
        )
        mom[1] = wet_here * (
            merid + time_step * (-coriolis * zonal - grad_y) + viscosity * laplace(1)
        )
        @pl.loop(0, rows // 32)
        def _(block):
            span = pl.ds(pl.multiple_of(32 * block, 8), 32)
            wet_span = pl.ds(pl.multiple_of(32 * block + PAD, 8), 32)
            nutrient, phyto, zoo, detritus = [acc[i, span] for i in range(4)]
            speed = growth[span]
            step = bio_step * wet[wet_span]
            for _ in range(SUBSTEPS):
                uptake = speed * nutrient / (half_nutrient + jnp.abs(nutrient)) * phyto
                square = phyto * phyto
                grazing = zoo * square / (half_prey + square)
                nutrient_next = nutrient + step * (remin_rate * detritus - uptake)
                phyto_next = phyto + step * (uptake - grazing - phyto_loss * phyto)
                zoo_next = zoo + step * (graze_yield * grazing - zoo_loss * zoo)
                detritus = detritus + step * (
                    (1.0 - graze_yield) * grazing
                    + phyto_loss * phyto
                    + zoo_loss * zoo
                    - remin_rate * detritus
                )
                nutrient, phyto, zoo = nutrient_next, phyto_next, zoo_next
            for i, value in enumerate((nutrient, phyto, zoo, detritus)):
                acc[i, span] = value


    for number in (1, 2):
        rows_of_piece(number)

    @pl.when(jnp.logical_not(waits_east_west) | is_top)
    def _():
        finish()

    for number in range(3, len(pieces)):
        rows_of_piece(number)

    @pl.when(waits_east_west & has_north)
    def _():
        reply_east_west()
        along_longitude(carrying=True)
        finish()

    @pl.when(jnp.logical_not(waits_east_west))
    def _():
        forward(0, 1)

    for route, mine in enumerate(carries, 1):

        @pl.when(mine)
        def _():
            for number in relayed:
                if pieces[number][3] == route:
                    from_carrier(number).wait_send()

    to_right.wait_send()
    to_left.wait_send()
    for number in range(len(pieces)):
        piece(number, 0, 0, north).wait_send()

        @pl.when(has_south)
        def _():
            piece(number, 1, 1, south).wait_send()


def write_out(acc, heat, mom, otr, ots, ofl, sem):
    outs = [
        pltpu.make_async_copy(acc.at[0 : otr.shape[0]], otr, sem.at[0]),
        pltpu.make_async_copy(heat, ots, sem.at[1]),
        pltpu.make_async_copy(mom, ofl, sem.at[2]),
    ]
    for out in outs:
        out.start()
    for out in outs:
        out.wait()


def body(tracers, flow, temp_salt, wet):
    count, levels, height, breadth = tracers.shape
    rows = levels * height
    fields = count + 2
    entries = piece_list(count)
    pieces = len(entries)
    moored = sum(hi - lo for _, lo, hi, route in entries if route)
    f32 = jnp.float32
    field = pltpu.VMEM((rows, breadth), f32)
    padded = pltpu.VMEM((rows + 2 * PAD, breadth), f32)
    dma = pltpu.SemaphoreType.DMA
    anywhere = pl.BlockSpec(memory_space=pl.ANY)
    local = pl.BlockSpec(memory_space=pltpu.VMEM)
    pair = (2, rows, breadth)
    results = pl.pallas_call(
        kernel,
        out_shape=(
            pltpu.VMEM((fields, rows, breadth), f32),
            pltpu.VMEM(pair, f32),
            pltpu.VMEM(pair, f32),
        ),
        in_specs=[anywhere] * 4,
        out_specs=(local,) * 3,
        scratch_shapes=[
            pltpu.VMEM((fields, rows + 2 * PAD, breadth), f32),
            pltpu.VMEM((3, rows + 2 * PAD, breadth), f32),
            pltpu.VMEM((rows, breadth), jnp.int32),
            padded,
            pltpu.VMEM((2, fields, rows, breadth), f32),
            pltpu.VMEM((2, 3, levels, breadth), f32),
            pltpu.VMEM((2, 3, levels, breadth), f32),
            field,
            pltpu.VMEM(pair, f32),
            field,
            field,
            field,
            field,
            field,
            field,
            pltpu.VMEM((3, levels, breadth), f32),
            pltpu.VMEM((3, levels, breadth), f32),
            field,
            field,
            pltpu.VMEM((3, rows + 2 * PAD, breadth), f32),
            pltpu.VMEM((3, rows + 2 * PAD, breadth), f32),
            pltpu.VMEM((3, rows, breadth), f32),
            pltpu.VMEM((max(1, moored), rows, breadth), f32),
            dma((4,)),
            dma((2,)),
            dma((2,)),
            dma((2, pieces)),
            dma((2, pieces)),
            dma((pieces,)),
            dma((pieces,)),
            pltpu.SemaphoreType.REGULAR((3,)),
        ],
        compiler_params=pltpu.CompilerParams(collective_id=0, has_side_effects=True),
        name="step",
    )(
        tracers.reshape(count, rows, breadth),
        flow.reshape(3, rows, breadth),
        temp_salt.reshape(2, rows, breadth),
        wet.reshape(rows, breadth),
    )
    outs = pl.pallas_call(
        write_out,
        out_shape=(
            jax.ShapeDtypeStruct((count, rows, breadth), f32),
            jax.ShapeDtypeStruct(pair, f32),
            jax.ShapeDtypeStruct(pair, f32),
        ),
        in_specs=[local] * 3,
        out_specs=(anywhere,) * 3,
        scratch_shapes=[dma((3,))],
        name="write_out",
    )(*(pltpu.with_memory_space_constraint(value, pltpu.VMEM) for value in results))
    return tuple(out.reshape(-1, levels, height, breadth) for out in outs)


def solution(mesh):
    four = P(None, None, "gy", ("grp", "gx"))
    return jax.shard_map(
        body,
        mesh=mesh,
        in_specs=(four, four, four, P(None, "gy", ("grp", "gx"))),
        out_specs=(four, four, four),
        check_vma=False,
    )
```

```python
import functools

import jax
import jax.numpy as jnp
from jax import lax
from jax.experimental import pallas as pl
from jax.experimental.pallas import tpu as pltpu
from jax.sharding import PartitionSpec as P

SUBSTEPS = 4
light_water = 0.04
light_chloro = 0.06
rho_temp = -0.2
rho_salt = 0.8
time_step = 0.02
coriolis = 0.4
viscosity = 0.1
heat_gain = 4.0
photic_halfway_level = 0.2
highest_division_speed = 1.5
half_nutrient = 0.5
half_prey = 0.3
phyto_loss = 0.05
zoo_loss = 0.1
graze_yield = 0.3
remin_rate = 0.15
bio_step = 0.25
thermal_multiplier = 0.063

LANES = 128
PAD = 8
OUT_PARTS = 6


EDGE, TEMP_SALT = "edge", "temp_salt"


def piece_list(tracers):
    pieces = [(EDGE, 0, 0, 0), (TEMP_SALT, tracers, tracers + 2, 0)]
    plan = ((3, 1), (3, 2), (2, 3), None, (1, 0), (2, 1), (2, 2), (tracers, 3))
    start = 4
    for entry in plan:
        if entry is None:
            pieces.append(("tracers", 0, 4, 0))
            continue
        size, route = entry
        stop = min(tracers, start + size)
        if stop > start:
            pieces.append(("tracers", start, stop, route))
        start = stop
    return pieces


def minmod(former, latter):
    return jnp.maximum(
        jnp.minimum(former, latter), jnp.minimum(jnp.maximum(former, latter), 0.0)
    )


def face_terms(speed):
    return jnp.where(speed > 0.0, 0.5 * (1.0 - speed), -0.5 * (1.0 + speed))


def upwind(speed, weight, low, high, low_slope, high_slope):
    forward = speed > 0.0
    value = jnp.where(forward, low, high)
    slope = jnp.where(forward, low_slope, high_slope)
    return speed * (value + weight * slope)


def in_batches(lo, hi, width, work):
    steps = (hi - lo) // width
    if steps == 1:
        work([lo + part for part in range(width)])
    elif steps > 1:
        pl.loop(0, steps)(lambda step: work([lo + width * step + part for part in range(width)]))
    if lo + steps * width < hi:
        work(list(range(lo + steps * width, hi)))


def running_sum(values, stride):
    rows = values.shape[0]
    index = lax.broadcasted_iota(jnp.int32, values.shape, 0)
    shift = stride
    while shift < rows:
        moved = pltpu.roll(values, shift, 0)
        values = values + jnp.where(index >= shift, moved, 0.0)
        shift *= 2
    return values


def kernel(
    tr,
    fl,
    ts,
    wt,
    acc,
    heat,
    mom,
    q,
    flow,
    wet_raw,
    wet,
    halo,
    edge_out,
    edge,
    pack,
    pack_in,
    line,
    side,
    cz,
    hz,
    cx,
    hx,
    cy,
    hy,
    growth,
    absorbed,
    fz,
    sz,
    nbr,
    transit,
    load_sem,
    pack_send,
    pack_recv,
    send_sem,
    recv_sem,
    relay_send,
    relay_recv,
    go,
):
    tracers = tr.shape[0]
    fields = tracers + 2
    rows = q.shape[1] - 2 * PAD
    levels = rows // 2
    temp, salt = tracers, tracers + 1
    pieces = piece_list(tracers)
    whole = slice(PAD, PAD + rows)

    grp, gx, gy = lax.axis_index("grp"), lax.axis_index("gx"), lax.axis_index("gy")
    n_grp, n_gx, n_gy = lax.axis_size("grp"), lax.axis_size("gx"), lax.axis_size("gy")
    lon, n_lon = grp * n_gx + gx, n_grp * n_gx

    def place(index):
        return index // n_gx, index % n_gx

    def depth(index):
        return (index % n_gx) // (n_gx // 2) * n_grp + index // n_gx

    right_lon = (lon + 1) % n_lon
    left_lon = (lon + n_lon - 1) % n_lon
    mirror_lon = n_lon - 1 - lon
    right, left = (*place(right_lon), gy), (*place(left_lon), gy)
    north, south = (grp, gx, jnp.minimum(gy + 1, n_gy - 1)), (grp, gx, jnp.maximum(gy - 1, 0))
    partner = (*place(mirror_lon), n_gy - 1)
    carrier_rows = (1, n_gy - 4, n_gy - 6)
    carriers = [(*place(mirror_lon), r) for r in carrier_rows]
    own_carriers = [(grp, gx, r) for r in carrier_rows]
    own_top = (grp, gx, n_gy - 1)
    is_top, has_south = gy == n_gy - 1, gy > 0
    has_north = gy < n_gy - 1
    here, over_right, over_left = depth(lon), depth(right_lon), depth(left_lon)
    early_right, early_left = here < over_right, here < over_left
    late_right, late_left = here > over_right, here > over_left
    early_fold = here < depth(mirror_lon)
    answers = is_top & early_fold
    opens = is_top & jnp.logical_not(early_fold)
    carries = [gy == r for r in carrier_rows]
    relays = carries[0] | carries[1] | carries[2]
    waits_east_west = early_right | early_left
    mesh_id = pl.DeviceIdType.MESH

    barrier = pltpu.get_barrier_semaphore()

    def greet(condition, other):
        @pl.when(condition)
        def _():
            pl.semaphore_signal(barrier, inc=1, device_id=other, device_id_type=mesh_id)

    greet(answers, partner)
    for other in own_carriers:
        greet(is_top, other)
    greet(relays & early_fold, partner)
    greet(has_north, north)
    greet(has_south, south)
    greet(jnp.logical_not(late_right), right)
    greet(jnp.logical_not(late_left), left)

    def one(condition):
        return jnp.where(condition, 1, 0)

    expected = one(has_north) + one(has_south) + one(opens) * 4 + one(relays)
    expected += one(jnp.logical_not(early_right)) + one(jnp.logical_not(early_left))

    loads = [
        pltpu.make_async_copy(wt, wet_raw, load_sem.at[0]),
        pltpu.make_async_copy(fl, flow.at[:, whole], load_sem.at[1]),
        pltpu.make_async_copy(ts, q.at[tracers:fields, whole], load_sem.at[2]),
    ]
    cuts = sorted({0, *(cut for cut in (6, 12, 18) if cut < tracers), tracers})
    for number, (lo, hi) in enumerate(zip(cuts[:-1], cuts[1:])):
        source, target = tr.at[lo:hi], q.at[lo:hi, whole]
        loads.append(pltpu.make_async_copy(source, target, load_sem.at[3 + number]))
    for load in loads:
        load.start()

    def piece(number, way, slot, device):
        kind, lo, hi, _ = pieces[number]
        if kind == EDGE:
            source, target = edge_out.at[way], edge.at[slot]
        elif kind == TEMP_SALT:
            source, target = ts, halo.at[slot, lo:hi]
        else:
            source, target = tr.at[lo:hi], halo.at[slot, lo:hi]
        return pltpu.make_async_remote_copy(
            source,
            target,
            send_sem.at[way, number],
            recv_sem.at[slot, number],
            device,
            mesh_id,
        )

    relayed = [number for number, entry in enumerate(pieces) if entry[3]]
    berth, total = {}, 0
    for number in relayed:
        berth[number] = total
        total += pieces[number][2] - pieces[number][1]

    def to_carrier(number):
        _, lo, hi, _ = pieces[number]
        start = berth[number]
        return pltpu.make_async_remote_copy(
            tr.at[lo:hi],
            transit.at[start : start + hi - lo],
            send_sem.at[0, number],
            relay_recv.at[number],
            carriers[pieces[number][3] - 1],
            mesh_id,
        )

    def from_carrier(number):
        _, lo, hi, _ = pieces[number]
        start = berth[number]
        return pltpu.make_async_remote_copy(
            transit.at[start : start + hi - lo],
            halo.at[1, lo:hi],
            relay_send.at[number],
            recv_sem.at[1, number],
            own_top,
            mesh_id,
        )

    def send(number):
        @pl.when(has_north)
        def _():
            piece(number, 0, 0, north).start()

        @pl.when(has_south)
        def _():
            piece(number, 1, 1, south).start()

    def open_fold(number):
        @pl.when(opens)
        def _():
            if number in berth:
                to_carrier(number).start()
            else:
                piece(number, 0, 1, partner).start()

    pl.semaphore_wait(barrier, expected)

    def permit(condition, slot, other):
        @pl.when(condition)
        def _():
            pl.semaphore_signal(go.at[slot], inc=1, device_id=other, device_id_type=mesh_id)

    permit(opens, 2, partner)
    permit(relays & jnp.logical_not(early_fold), 3, own_top)
    permit(late_right, 1, right)
    permit(late_left, 0, left)
    for number in (1, *relayed[: len(carriers)]):
        open_fold(number)

    lane = lax.broadcasted_iota(jnp.int32, (rows, LANES), 1)
    quad = lane // 4
    spot = lane % 4
    first, last = lane == 0, lane == LANES - 1

    def row_of(ref, r):
        return ref[pl.ds(r, levels, stride=2), :]

    loads[0].wait()
    loads[1].wait()
    wet[whole] = wet_raw[...].astype(jnp.float32)
    for way, r in ((0, 1), (1, 0)):
        for slot in range(2):
            edge_out[way, slot] = flow[slot, pl.ds(PAD + r, levels, stride=2), :]
        edge_out[way, 2] = wet[pl.ds(PAD + r, levels, stride=2), :]

    zeros = jnp.zeros((PAD, LANES), jnp.float32)
    below = slice(PAD + rows, PAD + rows + PAD)
    scraps = [ref.at[part] for ref in (fz, sz) for part in range(3)]
    for pads in (wet, flow.at[0], *scraps):
        pads[0:PAD] = zeros
        pads[below] = zeros

    @pl.loop(0, fields)
    def _(f):
        q[f, 0:PAD] = zeros
        q[f, below] = zeros

    open_fold(0)
    def take(step, packed):
        for part in range(3):
            f = 3 * step + part
            turned = pltpu.roll(q[f, whole], 4 * f + 2, 1)
            packed = jnp.where(quad == f, turned, packed)
        return packed

    packed = jnp.zeros((rows, LANES), jnp.float32)
    done = 0
    for number, cut in enumerate(cuts[1:]):
        loads[3 + number].wait()
        if cut == tracers:
            loads[2].wait()
            cut = fields
        packed = lax.fori_loop(done, cut // 3, take, packed)
        done = cut // 3

    for slot in range(3):
        f = fields + slot
        packed = jnp.where(quad == f, pltpu.roll(flow[slot, whole], 4 * f + 2, 1), packed)
    f = fields + 3
    packed = jnp.where(quad == f, pltpu.roll(wet[whole], 4 * f + 2, 1), packed)
    pack[...] = packed

    to_right = pltpu.make_async_remote_copy(
        pack, pack_in.at[0], pack_send.at[0], pack_recv.at[0], right, mesh_id
    )
    to_left = pltpu.make_async_remote_copy(
        pack, pack_in.at[1], pack_send.at[1], pack_recv.at[1], left, mesh_id
    )

    @pl.when(jnp.logical_not(early_right))
    def _():
        to_right.start()

    @pl.when(jnp.logical_not(early_left))
    def _():
        to_left.start()

    for number in range(len(pieces)):
        if number not in (0, 1, *relayed[: len(carriers)]):
            open_fold(number)

    @pl.when(opens)
    def _():
        pl.semaphore_wait(go.at[3], len(carriers))

    permit(opens, 4, partner)
    for number in range(len(pieces)):
        send(number)

    @pl.when(jnp.logical_not(has_south))
    def _():
        edge[0] = jnp.zeros((3, levels, LANES), jnp.float32)

        @pl.loop(0, fields)
        def _(f):
            halo[0, f] = jnp.zeros((rows, LANES), jnp.float32)

    mirror = LANES - 1 - lax.broadcasted_iota(jnp.int32, (levels, LANES), 1)

    def flip(values):
        return jnp.take_along_axis(values, mirror, axis=1)

    def await_piece(number):
        kind, lo, hi, _ = pieces[number]

        @pl.when(has_south)
        def _():
            piece(number, 0, 0, south).wait_recv()

        piece(number, 1, 1, south).wait_recv()

        @pl.when(is_top)
        def _():
            if kind == EDGE:
                edge[1, 0] = -flip(edge[1, 0])
                edge[1, 1] = -flip(edge[1, 1])
                edge[1, 2] = flip(edge[1, 2])
            else:

                def turn(batch):
                    rims = [(halo.at[1, f], r) for f in batch for r in range(2)]
                    turned = [flip(row_of(there, r)) for there, r in rims]
                    for (there, r), value in zip(rims, turned):
                        there[pl.ds(1 - r, levels, stride=2), :] = value

                in_batches(lo, hi, 2, turn)

    wet_here = wet[whole]

    speed = 0.5 * (flow[0, whole] + flow[0, PAD + 2 : PAD + 2 + rows])
    speed = speed * wet_here * wet[PAD + 2 : PAD + 2 + rows]
    cz[...] = speed
    hz[...] = face_terms(speed)

    attenuation = wet_here * (light_water + light_chloro * q[1, whole])
    light_top = jnp.exp(-(running_sum(attenuation, 2) - attenuation))
    absorbed[...] = light_top * (1.0 - jnp.exp(-attenuation))
    growth[...] = (
        highest_division_speed
        * jnp.exp(thermal_multiplier * q[temp, whole])
        * light_top
        / (photic_halfway_level + light_top)
    )

    def beyond(ref, f):
        return pltpu.roll(ref[...], LANES - 2 - 4 * f, 1)

    def east(values, outer):
        return pltpu.roll(jnp.where(first, outer, values), LANES - 1, 1)

    def west(values, outer):
        return pltpu.roll(jnp.where(last, outer, values), 1, 1)

    def along_levels(batch):
        values = [q[f, whole] for f in batch]
        deeper = [q[f, PAD + 2 : PAD + 2 + rows] for f in batch]
        slopes = [
            minmod(d - v, v - q[f, PAD - 2 : PAD - 2 + rows])
            for d, v, f in zip(deeper, values, batch)
        ]
        for part, slope in enumerate(slopes):
            sz[part, whole] = slope
        fluxes = [
            upwind(cz[...], hz[...], v, d, slope, sz[part, PAD + 2 : PAD + 2 + rows])
            for part, (v, d, slope) in enumerate(zip(values, deeper, slopes))
        ]
        for part, flux in enumerate(fluxes):
            fz[part, whole] = flux
        for part, (f, v, flux) in enumerate(zip(batch, values, fluxes)):
            acc[f] = v - (flux - fz[part, PAD - 2 : PAD - 2 + rows])

    in_batches(0, fields, 3, along_levels)

    def reply_east_west():
        @pl.when(early_right)
        def _():
            pl.semaphore_wait(go.at[0], 1)
            to_right.start()

        @pl.when(early_left)
        def _():
            pl.semaphore_wait(go.at[1], 1)
            to_left.start()

    def forward(part, parts):
        for route, mine in enumerate(carries, 1):
            routed = [number for number in relayed if pieces[number][3] == route]

            @pl.when(mine)
            def _():
                for number in routed[part * len(routed) // parts : (part + 1) * len(routed) // parts]:
                    to_carrier(number).wait_recv()
                    from_carrier(number).start()

    def along_longitude(carrying=False):
        if carrying:
            forward(0, 2)
        to_right.wait_recv()
        to_left.wait_recv()
        own = pack[...]
        lines = jnp.where(spot < 2, pack_in[0], pack_in[1])
        line[...] = lines
        wet_here = wet[whole]
        eastward = flow[2, whole]
        outer_wet = beyond(line, fields + 3)
        outer_flow = beyond(line, fields + 2)
        wet_east, wet_west = east(wet_here, outer_wet), west(wet_here, outer_wet)
        speed = 0.5 * (eastward + east(eastward, outer_flow)) * wet_here * wet_east
        cx[...] = speed
        hx[...] = face_terms(speed)
        entry = 0.5 * (west(eastward, outer_flow) + eastward) * wet_west * wet_here
        entry = jnp.broadcast_to(entry[:, 0:1], (rows, LANES))

        low_line = jnp.where(spot < 2, lines, own)
        low_next = pltpu.roll(low_line, LANES - 1, 1)
        gap = low_next - low_line
        low_slope = minmod(gap, pltpu.roll(gap, 1, 1))
        entry_flux = upwind(
            entry,
            face_terms(entry),
            low_line,
            low_next,
            low_slope,
            pltpu.roll(low_slope, LANES - 1, 1),
        )
        high_line = jnp.where(spot < 2, own, lines)
        gap = pltpu.roll(high_line, LANES - 1, 1) - high_line
        high_slope = minmod(gap, pltpu.roll(gap, 1, 1))
        side[...] = jnp.where(spot == 1, entry_flux, high_slope)

        def some_fields(step):
            batch = [3 * step + part for part in range(3)]
            before = [acc[f] for f in batch]
            values = [q[f, whole] for f in batch]
            outers = [beyond(line, f) for f in batch]
            sides = [beyond(side, f) for f in batch]
            nexts = [east(v, o) for v, o in zip(values, outers)]
            slopes = [
                minmod(n - v, v - west(v, o)) for n, v, o in zip(nexts, values, outers)
            ]
            fluxes = [
                upwind(cx[...], hx[...], v, n, slope, east(slope, outer_side))
                for v, n, slope, outer_side in zip(values, nexts, slopes, sides)
            ]
            for f, old, flux, outer_side in zip(batch, before, fluxes, sides):
                acc[f] = old - (flux - west(flux, outer_side))

        parts, batches = 2 if carrying else 1, fields // 3
        for part in range(parts):
            pl.loop(part * batches // parts, (part + 1) * batches // parts)(some_fields)
            if carrying and part == 0:
                forward(1, 2)

    @pl.when(jnp.logical_not(waits_east_west))
    def _():
        along_longitude()

    @pl.when(waits_east_west & is_top)
    def _():
        reply_east_west()

    @pl.when(answers)
    def _():
        pl.semaphore_wait(go.at[2], 1)
        for number in range(len(pieces)):
            if number not in berth:
                piece(number, 0, 1, partner).start()
        pl.semaphore_wait(go.at[4], 1)
        for number in relayed:
            to_carrier(number).start()

    @pl.when(waits_east_west & is_top)
    def _():
        along_longitude()

    await_piece(0)
    own_rows = [wet[pl.ds(PAD + r, levels, stride=2), :] for r in range(2)]
    wets = [edge[0, 2]] + own_rows + [edge[1, 2]]
    flows = [edge[0, 1]]
    flows += [flow[1, pl.ds(PAD + r, levels, stride=2), :] for r in range(2)]
    flows += [edge[1, 1]]
    for face in range(3):
        speed = 0.5 * (flows[face] + flows[face + 1]) * wets[face] * wets[face + 1]
        cy[face] = speed
        hy[face] = face_terms(speed)

    def across(f):
        results = []
        for block in range(levels // 8):
            span = slice(8 * block, 8 * block + 8)

            def load(ref, start, r):
                return ref[pl.ds(start + 16 * block + r, 8, stride=2), :]

            here = q.at[f]
            values = [load(halo.at[0, f], 0, 0), load(halo.at[0, f], 0, 1)]
            values += [load(here, PAD, 0), load(here, PAD, 1)]
            values += [load(halo.at[1, f], 0, 0), load(halo.at[1, f], 0, 1)]
            gaps = [values[i + 1] - values[i] for i in range(5)]
            slopes = [minmod(gaps[i + 1], gaps[i]) for i in range(4)]
            fluxes = [
                upwind(
                    cy[i, span],
                    hy[i, span],
                    values[i + 1],
                    values[i + 2],
                    slopes[i],
                    slopes[i + 1],
                )
                for i in range(3)
            ]
            for r in range(2):
                target = (f, pl.ds(16 * block + r, 8, stride=2), slice(None))
                results.append((target, acc[target] - (fluxes[r + 1] - fluxes[r])))
        return results

    def across_all(batch):
        for target, value in [entry for f in batch for entry in across(f)]:
            acc[target] = value

    def rows_of_piece(number):
        await_piece(number)
        _, lo, hi, _ = pieces[number]

        in_batches(lo, hi, 2, across_all)

    def momentum():
        wet_here = wet[whole]
        outer_wet = beyond(line, fields + 3)
        wet_east, wet_west = east(wet_here, outer_wet), west(wet_here, outer_wet)
        heat[0] = acc[temp] + heat_gain * absorbed[...]
        heat[1] = acc[salt]

        def weigh(wetness, heat, salinity):
            return wetness * (rho_temp * heat + rho_salt * salinity)

        def pressure_of(density, stride):
            return running_sum(density, stride) - 0.5 * density

        press = pressure_of(weigh(wet_here, q[temp, whole], q[salt, whole]), 2)
        outer_press = pressure_of(weigh(outer_wet, beyond(line, temp), beyond(line, salt)), 2)
        press_south = pressure_of(
            weigh(edge[0, 2], row_of(halo.at[0, temp], 1), row_of(halo.at[0, salt], 1)), 1
        )
        press_north = pressure_of(
            weigh(edge[1, 2], row_of(halo.at[1, temp], 0), row_of(halo.at[1, salt], 0)), 1
        )
        nbr[2] = press

        def spread(slot, own_ref, start, lower, upper):
            nbr[0, pl.ds(0, levels, stride=2), :] = lower
            nbr[0, pl.ds(1, levels, stride=2), :] = own_ref[pl.ds(start, levels, stride=2), :]
            nbr[1, pl.ds(0, levels, stride=2), :] = own_ref[pl.ds(start + 1, levels, stride=2), :]
            nbr[1, pl.ds(1, levels, stride=2), :] = upper
            return nbr[1], nbr[0]

        wet_north, wet_south = spread(0, wet, PAD, edge[0, 2], edge[1, 2])
        near_wet = (wet_east, wet_west, wet_north, wet_south)
        press_n, press_s = spread(1, nbr.at[2], 0, press_south, press_north)
        near = (east(press, outer_press), west(press, outer_press), press_n, press_s)
        near = [w * p + (1.0 - w) * press for w, p in zip(near_wet, near)]
        grad_x = 0.5 * (near[0] - near[1])
        grad_y = 0.5 * (near[2] - near[3])

        def laplace(slot):
            values = flow[slot, whole]
            outer = beyond(line, fields + slot)
            up, down = spread(slot, flow.at[slot], PAD, edge[0, slot], edge[1, slot])
            near_values = (east(values, outer), west(values, outer), up, down)
            total = near_wet[0] * near_values[0]
            for w, value in zip(near_wet[1:], near_values[1:]):
                total = total + w * value
            return total - 4.0 * values

        zonal, merid = flow[0, whole], flow[1, whole]
        mom[0] = wet_here * (
            zonal + time_step * (coriolis * merid - grad_x) + viscosity * laplace(0)
        )
        mom[1] = wet_here * (
            merid + time_step * (-coriolis * zonal - grad_y) + viscosity * laplace(1)
        )

    def plankton():
        @pl.loop(0, rows // 32)
        def _(block):
            span = pl.ds(pl.multiple_of(32 * block, 8), 32)
            wet_span = pl.ds(pl.multiple_of(32 * block + PAD, 8), 32)
            nutrient, phyto, zoo, detritus = [acc[i, span] for i in range(4)]
            speed = growth[span]
            step = bio_step * wet[wet_span]
            for _ in range(SUBSTEPS):
                uptake = speed * nutrient / (half_nutrient + jnp.abs(nutrient)) * phyto
                square = phyto * phyto
                grazing = zoo * square / (half_prey + square)
                nutrient_next = nutrient + step * (remin_rate * detritus - uptake)
                phyto_next = phyto + step * (uptake - grazing - phyto_loss * phyto)
                zoo_next = zoo + step * (graze_yield * grazing - zoo_loss * zoo)
                detritus = detritus + step * (
                    (1.0 - graze_yield) * grazing
                    + phyto_loss * phyto
                    + zoo_loss * zoo
                    - remin_rate * detritus
                )
                nutrient, phyto, zoo = nutrient_next, phyto_next, zoo_next
            for i, value in enumerate((nutrient, phyto, zoo, detritus)):
                acc[i, span] = value


    rows_of_piece(1)

    @pl.when(jnp.logical_not(waits_east_west) | is_top)
    def _():
        momentum()


    plankton_piece = [kind == "tracers" and lo == 0 for kind, lo, _, _ in pieces].index(True)
    for number in range(2, plankton_piece + 1):
        rows_of_piece(number)

    @pl.when(jnp.logical_not(waits_east_west) | is_top)
    def _():
        plankton()

    for number in range(plankton_piece + 1, len(pieces)):
        rows_of_piece(number)

    @pl.when(waits_east_west & has_north)
    def _():
        reply_east_west()
        along_longitude(carrying=True)
        momentum()
        plankton()

    @pl.when(jnp.logical_not(waits_east_west))
    def _():
        forward(0, 1)

    for route, mine in enumerate(carries, 1):

        @pl.when(mine)
        def _():
            for number in relayed:
                if pieces[number][3] == route:
                    from_carrier(number).wait_send()

    to_right.wait_send()
    to_left.wait_send()
    for number in range(len(pieces)):
        piece(number, 0, 0, north).wait_send()

        @pl.when(has_south)
        def _():
            piece(number, 1, 1, south).wait_send()


def write_out(acc, heat, mom, otr, ots, ofl, sem):
    count = otr.shape[0]
    cuts = [count * part // OUT_PARTS for part in range(OUT_PARTS + 1)]
    outs = [
        pltpu.make_async_copy(acc.at[lo:hi], otr.at[lo:hi], sem.at[2 + number])
        for number, (lo, hi) in enumerate(zip(cuts[:-1], cuts[1:]))
    ]
    outs.append(pltpu.make_async_copy(heat, ots, sem.at[0]))
    outs.append(pltpu.make_async_copy(mom, ofl, sem.at[1]))
    for out in outs:
        out.start()
    for out in outs:
        out.wait()


def body(tracers, flow, temp_salt, wet):
    count, levels, height, breadth = tracers.shape
    rows = levels * height
    fields = count + 2
    entries = piece_list(count)
    pieces = len(entries)
    moored = sum(hi - lo for _, lo, hi, route in entries if route)
    f32 = jnp.float32
    field = pltpu.VMEM((rows, breadth), f32)
    padded = pltpu.VMEM((rows + 2 * PAD, breadth), f32)
    dma = pltpu.SemaphoreType.DMA
    anywhere = pl.BlockSpec(memory_space=pl.ANY)
    local = pl.BlockSpec(memory_space=pltpu.VMEM)
    pair = (2, rows, breadth)
    results = pl.pallas_call(
        kernel,
        out_shape=(
            pltpu.VMEM((fields, rows, breadth), f32),
            pltpu.VMEM(pair, f32),
            pltpu.VMEM(pair, f32),
        ),
        in_specs=[anywhere] * 4,
        out_specs=(local,) * 3,
        scratch_shapes=[
            pltpu.VMEM((fields, rows + 2 * PAD, breadth), f32),
            pltpu.VMEM((3, rows + 2 * PAD, breadth), f32),
            pltpu.VMEM((rows, breadth), jnp.int32),
            padded,
            pltpu.VMEM((2, fields, rows, breadth), f32),
            pltpu.VMEM((2, 3, levels, breadth), f32),
            pltpu.VMEM((2, 3, levels, breadth), f32),
            field,
            pltpu.VMEM(pair, f32),
            field,
            field,
            field,
            field,
            field,
            field,
            pltpu.VMEM((3, levels, breadth), f32),
            pltpu.VMEM((3, levels, breadth), f32),
            field,
            field,
            pltpu.VMEM((3, rows + 2 * PAD, breadth), f32),
            pltpu.VMEM((3, rows + 2 * PAD, breadth), f32),
            pltpu.VMEM((3, rows, breadth), f32),
            pltpu.VMEM((max(1, moored), rows, breadth), f32),
            dma((7,)),
            dma((2,)),
            dma((2,)),
            dma((2, pieces)),
            dma((2, pieces)),
            dma((pieces,)),
            dma((pieces,)),
            pltpu.SemaphoreType.REGULAR((5,)),
        ],
        compiler_params=pltpu.CompilerParams(collective_id=0, has_side_effects=True),
        name="step",
    )(
        tracers.reshape(count, rows, breadth),
        flow.reshape(3, rows, breadth),
        temp_salt.reshape(2, rows, breadth),
        wet.reshape(rows, breadth),
    )
    outs = pl.pallas_call(
        write_out,
        out_shape=(
            jax.ShapeDtypeStruct((count, rows, breadth), f32),
            jax.ShapeDtypeStruct(pair, f32),
            jax.ShapeDtypeStruct(pair, f32),
        ),
        in_specs=[local] * 3,
        out_specs=(anywhere,) * 3,
        scratch_shapes=[dma((2 + OUT_PARTS,))],
        name="write_out",
    )(*(pltpu.with_memory_space_constraint(value, pltpu.VMEM) for value in results))
    return tuple(out.reshape(-1, levels, height, breadth) for out in outs)


def solution(mesh):
    four = P(None, None, "gy", ("grp", "gx"))
    return jax.shard_map(
        body,
        mesh=mesh,
        in_specs=(four, four, four, P(None, "gy", ("grp", "gx"))),
        out_specs=(four, four, four),
        check_vma=False,
    )
```
